32 devices in a mesh: grp: 2 (over y), doc: 4 (over x, core), voc: 4 (over z).
Axes of the slice: x: 2, y: 2, z: 4, core: 2. Of those that a mesh axis runs over, the one named last changes fastest.
Arguments:
- hidden: bfloat16 [48, 256, 768], P(('grp', 'doc')), parts along dimension 0, may hold values from -6 to 6
- lengths: int32 [48], P(('grp', 'doc')), parts along dimension 0, may hold values from 1 to 256, 3840 in all
- w_trans: bfloat16 [768, 768], replicated, may hold values from -0.21875 to 0.21875
- b_trans: float32 [768], replicated, may hold values from -3 to 3
- ln_gain: float32 [768], replicated, may hold values from 0.5 to 1.5
- ln_bias: float32 [768], replicated, may hold values from -3 to 3
- w_decode: bfloat16 [768, 30720], P(None, 'voc'), may hold values from -0.21875 to 0.21875
- b_decode: float32 [30720], P('voc'), may hold values from -5 to 5
- query_ids: int32 [2048, 32], P('grp'), parts along dimension 0, may hold values from 0 to 30719
- query_wts: int32 [2048, 32], P('grp'), parts along dimension 0, may hold values from 1 to 100
Outputs:
- scores: float32 [48, 1024], P(('grp', 'voc'), 'doc'), parts along dimension 0
The draws below stay inside these ranges and needn't reach their ends.
There are 2 independent parts, one for each index of `grp`. The reference program is written for one: setup_inputs(seed, part) draws one part's arguments, and reference() takes and returns one part's arrays. A program takes and returns all parts, laid end to end along the dimension named above; an argument that names none is the same for every part. Nothing has to cross between parts.
Inputs may be any that keep to these rules, and one draw needn't show every extreme that they name: Every passage has at least one live token and the longest has exactly 256. Within each grp group the 24 lengths sum to 3840; over the whole array, which holds both groups, the sum is twice that.
All inputs are finite; a program needn't handle non-finite values.
Results may differ from the reference program's by a relative error of at most 0.0003.
Values sent between devices are 32-bit elements; how exact they have to be, the bound alone decides.
A program may use at most 64 MiB of HBM per device.

```python
import math
import jax
import jax.numpy as jnp
import numpy as np
from jax import lax

D = 768
V = 30720
L = 256
QT = 32
P_SIZE = 24
Q = 1024


def plant(result, stream_key, smallest, largest):
    index_at = [jax.random.randint(jax.random.fold_in(stream_key, axis), (), 0, length) for axis, length in enumerate(result.shape)]
    main_axis = result.shape.index(max(result.shape))
    next_to = index_at[:main_axis] + [(index_at[main_axis] + 1) % result.shape[main_axis]] + index_at[main_axis + 1:]
    return result.at[tuple(index_at)].set(smallest).at[tuple(next_to)].set(largest)


def levels(stream_key, dims, cuts, least, top_value):
    gain, own = 1.0, jax.random.fold_in(stream_key, 6)
    for position, parts in cuts:
        steps = jnp.exp(jax.random.uniform(jax.random.fold_in(own, position), (parts,), jnp.float32, least / len(cuts), top_value / len(cuts)))
        gain = gain * jnp.repeat(steps, dims[position] // parts).reshape([-1 if axis == position else 1 for axis in range(len(dims))])
    return gain


def length_profile(number_of, total, limit, lean):
    loads = [(1 << 20) // math.isqrt(standing ** lean) + 1 for standing in range(2, number_of + 1)]
    spare, counts = total - limit - (number_of - 1), [1] * (number_of - 1)
    while spare > 0:
        free = [i for i in range(number_of - 1) if counts[i] < limit]
        pool, budget = sum([loads[i] for i in free]), spare
        for i in free:
            extra = min(limit - counts[i], max(1, budget * loads[i] // pool), spare)
            counts[i] = counts[i] + extra
            spare = spare - extra
    return np.array([limit] + counts)


def ragged(own_key, count, total, reach, lean):
    if count == 2:
        one = jax.random.randint(own_key, (), max(1, total - reach), min(reach, total - 1) + 1)
        return jnp.stack([one, total - one])
    sizes = jnp.asarray(length_profile(count, total, reach, lean), jnp.int32)
    twos = (count - 1) // 2
    source_of, sink = sizes[1:1 + 2 * twos:2], sizes[2:2 + 2 * twos:2]
    slack = jnp.minimum(source_of - 1, reach - sink)
    moved = jax.random.randint(jax.random.fold_in(own_key, 1), (twos,), 0, 1 << 20) % (slack + 1)
    sizes = sizes.at[1:1 + 2 * twos:2].set(source_of - moved).at[2:2 + 2 * twos:2].set(sink + moved)
    return sizes[jax.random.permutation(jax.random.fold_in(own_key, 2), count)]


def gaussian(stream_key, shape, scale, bound, shards=(), held_as=jnp.bfloat16):
    result = jax.random.normal(stream_key, shape, jnp.float32) * scale
    if len(shards) > 0:
        result = levels(stream_key, shape, shards, -0.22, 0.18) * result
    return jnp.clip(result, min=-bound, max=bound).astype(held_as)


def setup_inputs(seed: int = 0, part: int = 0) -> dict:
    splits = jax.random.split(jax.random.key(seed), 11)
    part_keys = jax.random.split(jax.random.fold_in(splits[10], part), 11)
    return {
        "hidden": gaussian(part_keys[0], (P_SIZE, L, D), 1.0, 6.0, ((0, 4),)),
        "lengths": ragged(part_keys[1], P_SIZE, P_SIZE * L * 5 // 8, L, 1).astype(jnp.int32),
        "w_trans": gaussian(splits[2], (D, D), D ** -0.5, 0.21875),
        "b_trans": gaussian(splits[3], (D,), 0.5, 3.0, (), jnp.float32),
        "ln_gain": jnp.clip(jax.random.uniform(splits[4], (D,), jnp.float32, 0.5, 1.5), 0.5, 1.5),
        "ln_bias": gaussian(splits[5], (D,), 0.5, 3.0, (), jnp.float32),
        "w_decode": gaussian(splits[6], (D, V), D ** -0.5, 0.21875, ((1, 4),)),
        "b_decode": gaussian(splits[7], (V,), 1.0, 5.0, ((0, 4),), jnp.float32),
        "query_ids": plant(jax.random.randint(part_keys[8], (Q, QT), 0, V), jax.random.fold_in(part_keys[8], 1), 0, V - 1).astype(jnp.int32),
        "query_wts": plant(jax.random.randint(part_keys[9], (Q, QT), 1, 101), jax.random.fold_in(part_keys[9], 1), 1, 100).astype(jnp.int32),
    }


eps = 1e-06
score_scale = 1.0 / 1024.0
dead_fill = -1e+30

def transform(hidden, w_trans, b_trans, ln_gain, ln_bias):
    count, length, width = hidden.shape
    flat = hidden.reshape(count * length, width)
    pre = jnp.dot(flat, w_trans, preferred_element_type=jnp.float32) + b_trans
    active = jax.nn.gelu(pre, approximate=False)
    centre = active - lax.optimization_barrier(jnp.mean(active, -1, keepdims=True))
    spread = lax.optimization_barrier(jnp.mean(centre * centre, -1, keepdims=True))
    normed = centre * lax.rsqrt(spread + eps) * ln_gain + ln_bias
    return normed.astype(jnp.bfloat16).reshape(count, length, width)

def reference(hidden, lengths, w_trans, b_trans, ln_gain, ln_bias, w_decode, b_decode, query_ids, query_wts):
    transformed = transform(hidden, w_trans, b_trans, ln_gain, ln_bias)
    decode_full = w_decode.astype(jnp.float32)

    def pool_rows(pair):
        passage, live = pair
        logits = jnp.dot(passage.astype(jnp.float32), decode_full) + b_decode
        inside = jnp.arange(passage.shape[0], dtype=jnp.int32)[:, None] < live
        top = lax.optimization_barrier(jnp.max(jnp.where(inside, logits, jnp.full_like(logits, dead_fill)), 0))
        return jnp.log1p(jnp.maximum(top, jnp.zeros_like(top)))
    impacts = lax.map(pool_rows, (transformed, lengths))
    weights = query_wts.astype(jnp.float32)
    picked = impacts[:, query_ids]
    return lax.optimization_barrier(jnp.sum(picked * weights[None], -1)) * score_scale
```

```python
import functools

import jax
import jax.numpy as jnp
from jax import lax
from jax.experimental import pallas as pl
from jax.experimental.pallas import tpu as pltpu
from jax.sharding import PartitionSpec as P

eps = 1e-06
score_scale = 1.0 / 1024.0
radix = 256
pad = 8


def tile_of(width):
    best = 128
    for tile in range(128, 1537, 128):
        if width % tile == 0:
            best = tile
    return best


def pieces_of(tile):
    if tile < 768 or tile % 256:
        return [tile]
    first = tile // 512 * 256
    return [cut for cut in (first, tile - first - 256, 256) if cut]


def encode_kernel(
    sizes, count, tile, lens, b_trans, gain, bias, b_decode, hidden, w_trans, w_decode, ids, wts,
    out, states, mix, decoder, kept, slots, own_ids, own_wts, hi_at, lo_at, weight_at, big, small,
    part, parts, live, shift, scale, offset, floor,
    load_sem, state_sem, decoder_sem, doc_send, doc_recv, voc_send, voc_recv
):
    docs, vocs = sizes
    length, features = hidden.shape[0] // count, hidden.shape[1]
    width = w_decode.shape[1]
    tiles = width // tile
    slots_per, queries = own_ids.shape
    per = radix // slots_per
    leads = width // radix
    grp, doc, voc = (lax.axis_index(name) for name in ("grp", "doc", "voc"))
    mesh_ids = pl.DeviceIdType.MESH

    def state_load(p):
        rows = pl.ds(p * length, length)
        return pltpu.make_async_copy(hidden.at[rows], states.at[rows], state_sem.at[p])

    def decoder_load(t):
        cut = pl.ds(pl.multiple_of(t * tile, tile), tile)
        return pltpu.make_async_copy(w_decode.at[:, cut], decoder.at[t], decoder_sem.at[t])

    rows = pl.ds(pl.multiple_of(doc * queries, queries), queries)
    smalls = [
        pltpu.make_async_copy(source, target, load_sem.at[i])
        for i, (source, target) in enumerate(
            [(lens, live), (b_trans, shift), (gain, scale), (bias, offset)]
        )
    ]
    later = [
        pltpu.make_async_copy(source, target, load_sem.at[4 + i])
        for i, (source, target) in enumerate(
            [(b_decode, floor), (ids.at[:, rows], own_ids), (wts.at[:, rows], own_wts)]
        )
    ]
    mix_load = pltpu.make_async_copy(w_trans, mix, load_sem.at[7])
    mix_load.start()
    state_load(0).start()
    for load in smalls:
        load.start()
    for p in range(1, count):
        state_load(p).start()
    for load in later:
        load.start()
    for t in range(tiles):
        decoder_load(t).start()

    barrier = pltpu.get_barrier_semaphore()
    across = [(grp, lax.rem(doc + j, docs), voc) for j in range(1, docs)]
    along = [(grp, doc, lax.rem(voc + j, vocs)) for j in range(1, vocs)]
    for peer in across + along:
        pl.semaphore_signal(barrier, inc=1, device_id=peer, device_id_type=mesh_ids)
    for load in smalls:
        load.wait()
    mix_load.wait()

    for p in range(count):
        state_load(p).wait()
        rows = pl.ds(p * length, length)
        pre = jnp.dot(states[rows, :], mix[...], preferred_element_type=jnp.float32)
        pre = pre + shift[...][None]
        twice = pre * (1.0 + lax.erf(pre * (0.5 ** 0.5)))
        centre = twice - jnp.mean(twice, -1, keepdims=True)
        spread = jnp.mean(centre * centre, -1, keepdims=True)
        normed = centre * lax.rsqrt(spread + 4.0 * eps) * scale[...][None] + offset[...][None]
        inside = lax.broadcasted_iota(jnp.int32, (length, features), 0) < live[p]
        kept[rows, :] = jnp.where(inside, normed, normed[0:1]).astype(jnp.bfloat16)

    for load in later:
        load.wait()
    local = own_ids[...] - voc * width
    lead = jnp.clip(local >> 8, -1, leads)
    spread_to = (
        lax.broadcasted_iota(jnp.int32, (slots_per, radix), 1) % slots_per
        == lax.broadcasted_iota(jnp.int32, (slots_per, radix), 0)
    ).astype(jnp.float32).astype(jnp.bfloat16)

    def widen(value):
        value = value.astype(jnp.float32).astype(jnp.bfloat16)
        return lax.dot_general(
            value, spread_to, (((0,), (0,)), ((), ())), preferred_element_type=jnp.float32
        )

    own = (
        lax.broadcasted_iota(jnp.int32, (queries, radix), 0) % per
        == lax.broadcasted_iota(jnp.int32, (queries, radix), 1) // slots_per
    )
    hi_at[...] = jnp.where(own, widen(lead), -1.0)
    lo_at[...] = jnp.where(own, widen(local & (radix - 1)), 0.0)
    weight_at[...] = widen(own_wts[...])

    spans = leads + leads % 2
    both = 2 * per

    def made_of(at):
        high, weight = hi_at[at, :], weight_at[at, :]
        low = jnp.sum(lo_at[at, :], 0, keepdims=True)
        left = jnp.concatenate(
            [jnp.where(high == float(i), weight, 0.0) for i in range(spans)], 0
        ).astype(jnp.bfloat16)
        digits = lax.broadcasted_iota(jnp.int32, (radix, radix), 0).astype(jnp.float32)
        right = jnp.where(digits == low, 1.0, 0.0).astype(jnp.bfloat16)
        return lax.dot_general(
            left, right, (((1,), (1,)), ((), ())), preferred_element_type=jnp.float32
        )

    def build(g):
        pair = [
            made_of(pl.ds(pl.multiple_of(g * both + i * per, per), per)) for i in range(2)
        ]
        at = pl.ds(pl.multiple_of(g * both, both), both)
        for i in range(leads):
            whole = jnp.concatenate([made[i * per:(i + 1) * per] for made in pair], 0)
            top = whole.astype(jnp.bfloat16)
            big[at, i * radix:(i + 1) * radix] = top
            small[at, i * radix:(i + 1) * radix] = (
                whole - top.astype(jnp.float32)
            ).astype(jnp.bfloat16)

    def share_copy(j, step, start, cut):
        mine = slots.at[doc, :, pl.ds(start, cut)]
        return pltpu.make_async_remote_copy(
            src_ref=mine, dst_ref=mine, send_sem=doc_send.at[j, step],
            recv_sem=doc_recv.at[j, step], device_id=across[j], device_id_type=mesh_ids
        )

    def decode(t, start, begin, cut, step):
        tops = []
        for p in range(count):
            logits = jnp.dot(
                kept[p * length:(p + 1) * length, :], decoder[t, :, begin:begin + cut],
                preferred_element_type=jnp.float32
            )
            tops.append(jnp.max(logits, 0, keepdims=True))
        tops.append(jnp.zeros((pad - count, cut), jnp.float32))
        best = jnp.concatenate(tops, 0) + floor[pl.ds(start, cut)][None]
        slots[doc, :, pl.ds(start, cut)] = jnp.log1p(jnp.maximum(best, 0.0))
        for j in range(len(across)):
            share_copy(j, step, start, cut).start()

    pl.semaphore_wait(barrier, len(across) + len(along))
    rounds = queries // both
    steady = tiles - 1
    inner = rounds // max(steady, 1)

    def decode_tile(t, _):
        decoder_load(t).wait()
        for i in range(inner):
            build(t * inner + i)
        decode(t, pl.multiple_of(t * tile, tile), 0, tile, t)
        return 0

    lax.fori_loop(0, steady, decode_tile, 0)
    for g in range(inner * steady, rounds):
        build(g)
    decoder_load(steady).wait()
    cuts, begin = [], 0
    for i, cut in enumerate(pieces_of(tile)):
        start = steady * tile + begin
        decode(steady, start, begin, cut, steady + i)
        cuts.append((steady + i, start, cut))
        begin += cut

    def contract(total, step, start, cut):
        for j in range(len(across)):
            share_copy(j, step, start, cut).wait()
        value = slots[:, :, pl.ds(start, cut)].reshape(docs * pad, cut)
        top = value.astype(jnp.bfloat16)
        rest = (value - top.astype(jnp.float32)).astype(jnp.bfloat16)
        pair = jnp.concatenate([top, rest], 0)
        for table in (big, small):
            total = total + lax.dot_general(
                pair, table[:, pl.ds(start, cut)], (((1,), (1,)), ((), ())),
                preferred_element_type=jnp.float32
            )
        return total

    total = jnp.zeros((2 * docs * pad, queries), jnp.float32)
    for t in range(steady):
        total = contract(total, t, t * tile, tile)
    for step, start, cut in cuts:
        total = contract(total, step, start, cut)
    total = (total[:docs * pad] + total[docs * pad:]) * score_scale
    part[...] = total.reshape(docs, pad, queries)

    share = docs // vocs
    copies = []
    for j, peer in enumerate(along):
        copy = pltpu.make_async_remote_copy(
            src_ref=part.at[pl.ds(peer[2] * share, share)], dst_ref=parts.at[j],
            send_sem=voc_send.at[j], recv_sem=voc_recv.at[j], device_id=peer,
            device_id_type=mesh_ids
        )
        copy.start()
        copies.append(copy)
    result = part[pl.ds(voc * share, share)]
    for j, copy in enumerate(copies):
        copy.wait()
        result = result + parts[j]
    for i in range(share):
        out[i * count:(i + 1) * count, :] = result[i, :count]


def shards(
    hidden, lengths, w_trans, b_trans, ln_gain, ln_bias, w_decode, b_decode, query_ids, query_wts
):
    docs, vocs = lax.axis_size("doc"), lax.axis_size("voc")
    count, length, features = hidden.shape
    width = w_decode.shape[1]
    tile = tile_of(width)
    tiles = width // tile
    steps = tiles - 1 + len(pieces_of(tile))
    terms = query_ids.shape[1]
    queries = query_ids.shape[0] // docs
    anywhere = pl.BlockSpec(memory_space=pl.ANY)
    inside = pl.BlockSpec(memory_space=pltpu.VMEM)
    lanes = pltpu.VMEM((queries, radix), jnp.float32)
    half = pltpu.VMEM((queries, width), jnp.bfloat16)
    row = pltpu.VMEM((features,), jnp.float32)
    queue = pltpu.SemaphoreType.DMA
    return pl.pallas_call(
        functools.partial(encode_kernel, (docs, vocs), count, tile),
        out_shape=jax.ShapeDtypeStruct((docs * count // vocs, queries), jnp.float32),
        in_specs=[anywhere] * 10,
        out_specs=inside,
        scratch_shapes=[
            pltpu.VMEM((count * length, features), jnp.bfloat16),
            pltpu.VMEM((features, features), jnp.bfloat16),
            pltpu.VMEM((tiles, features, tile), jnp.bfloat16),
            pltpu.VMEM((count * length, features), jnp.bfloat16),
            pltpu.VMEM((docs, pad, width), jnp.float32),
            pltpu.VMEM((terms, queries), jnp.int32),
            pltpu.VMEM((terms, queries), jnp.int32),
            lanes, lanes, lanes,
            half, half,
            pltpu.VMEM((docs, pad, queries), jnp.float32),
            pltpu.VMEM((vocs - 1, docs // vocs, pad, queries), jnp.float32),
            pltpu.SMEM((count,), jnp.int32),
            row, row, row,
            pltpu.VMEM((width,), jnp.float32),
            queue((8,)), queue((count,)), queue((tiles,)),
            queue((docs - 1, steps)), queue((docs - 1, steps)),
            queue((vocs - 1,)), queue((vocs - 1,)),
        ],
        compiler_params=pltpu.CompilerParams(
            collective_id=0, has_side_effects=True, vmem_limit_bytes=60 * 1024 * 1024
        ),
    )(
        lengths, b_trans, ln_gain, ln_bias, b_decode,
        hidden.reshape(count * length, features), w_trans, w_decode, query_ids.T, query_wts.T
    )


def solution(mesh):
    return jax.shard_map(
        shards,
        mesh=mesh,
        in_specs=(
            P(("grp", "doc"), None, None),
            P(("grp", "doc")),
            P(),
            P(),
            P(),
            P(),
            P(None, "voc"),
            P("voc"),
            P("grp", None),
            P("grp", None),
        ),
        out_specs=P(("grp", "voc"), "doc"),
        check_vma=False,
    )
```

```python
import functools

import jax
import jax.numpy as jnp
from jax import lax
from jax.experimental import pallas as pl
from jax.experimental.pallas import tpu as pltpu
from jax.sharding import PartitionSpec as P

eps = 1e-06
score_scale = 1.0 / 1024.0
radix = 256
pad = 8


def tile_of(width):
    best = 128
    for tile in range(128, 1537, 128):
        if width % tile == 0:
            best = tile
    return best


def pieces_of(tile):
    if tile < 768 or tile % 256:
        return [tile]
    first = tile // 512 * 256
    return [cut for cut in (first, tile - first - 256, 256) if cut]


def encode_kernel(
    sizes, count, tile, lens, b_trans, gain, bias, b_decode, hidden, w_trans, w_decode, ids, wts,
    out, states, mix, decoder, kept, slots, own_ids, own_wts, hi_at, lo_at, weight_at, big, small,
    part, parts, live, shift, scale, offset, floor,
    load_sem, state_sem, decoder_sem, doc_send, doc_recv, voc_send, voc_recv
):
    docs, vocs = sizes
    length, features = hidden.shape[0] // count, hidden.shape[1]
    width = w_decode.shape[1]
    tiles = width // tile
    slots_per, queries = own_ids.shape
    per = radix // slots_per
    leads = width // radix
    grp, doc, voc = (lax.axis_index(name) for name in ("grp", "doc", "voc"))
    mesh_ids = pl.DeviceIdType.MESH

    def state_load(p):
        rows = pl.ds(p * length, length)
        return pltpu.make_async_copy(hidden.at[rows], states.at[rows], state_sem.at[p])

    def decoder_load(t):
        cut = pl.ds(pl.multiple_of(t * tile, tile), tile)
        return pltpu.make_async_copy(w_decode.at[:, cut], decoder.at[t], decoder_sem.at[t])

    rows = pl.ds(pl.multiple_of(doc * queries, queries), queries)
    smalls = [
        pltpu.make_async_copy(source, target, load_sem.at[i])
        for i, (source, target) in enumerate(
            [(lens, live), (b_trans, shift), (gain, scale), (bias, offset)]
        )
    ]
    later = [
        pltpu.make_async_copy(source, target, load_sem.at[4 + i])
        for i, (source, target) in enumerate(
            [(b_decode, floor), (ids.at[:, rows], own_ids), (wts.at[:, rows], own_wts)]
        )
    ]
    mix_load = pltpu.make_async_copy(w_trans, mix, load_sem.at[7])
    mix_load.start()
    state_load(0).start()
    for load in smalls:
        load.start()
    for p in range(1, count):
        state_load(p).start()
    for load in later:
        load.start()
    barrier = pltpu.get_barrier_semaphore()
    cores = 2 - docs % 2
    chips = docs // cores
    chip, core = doc // cores, lax.rem(doc, cores)
    beside = cores - 1 - core

    def mate(shift, side):
        return cores * lax.rem(chip + shift, chips) + side

    links = [(mate(h, core), mate(chips - h, core)) for h in range(1, chips)]
    direct = len(links)
    if cores == 2:
        links += [(mate(h, beside), mate(chips - h, beside)) for h in range(chips)]
    along = [(grp, doc, lax.rem(voc + j, vocs)) for j in range(1, vocs)]
    for peer in [(grp, target, voc) for target, _ in links] + along:
        pl.semaphore_signal(barrier, inc=1, device_id=peer, device_id_type=mesh_ids)
    for load in smalls:
        load.wait()
    mix_load.wait()

    for p in range(count):
        state_load(p).wait()
        for t in range(p * tiles // count, (p + 1) * tiles // count):
            decoder_load(t).start()
        rows = pl.ds(p * length, length)
        pre = jnp.dot(states[rows, :], mix[...], preferred_element_type=jnp.float32)
        pre = pre + shift[...][None]
        twice = pre * (1.0 + lax.erf(pre * (0.5 ** 0.5)))
        centre = twice - jnp.mean(twice, -1, keepdims=True)
        spread = jnp.mean(centre * centre, -1, keepdims=True)
        normed = centre * lax.rsqrt(spread + 4.0 * eps) * scale[...][None] + offset[...][None]
        inside = lax.broadcasted_iota(jnp.int32, (length, features), 0) < live[p]
        kept[rows, :] = jnp.where(inside, normed, normed[0:1]).astype(jnp.bfloat16)

    for load in later:
        load.wait()
    local = own_ids[...] - voc * width
    lead = jnp.clip(local >> 8, -1, leads)
    spread_to = (
        lax.broadcasted_iota(jnp.int32, (slots_per, radix), 1) % slots_per
        == lax.broadcasted_iota(jnp.int32, (slots_per, radix), 0)
    ).astype(jnp.float32).astype(jnp.bfloat16)

    def widen(value):
        value = value.astype(jnp.float32).astype(jnp.bfloat16)
        return lax.dot_general(
            value, spread_to, (((0,), (0,)), ((), ())), preferred_element_type=jnp.float32
        )

    own = (
        lax.broadcasted_iota(jnp.int32, (queries, radix), 0) % per
        == lax.broadcasted_iota(jnp.int32, (queries, radix), 1) // slots_per
    )
    hi_at[...] = jnp.where(own, widen(lead), -1.0)
    lo_at[...] = jnp.where(own, widen(local & (radix - 1)), 0.0)
    weight_at[...] = widen(own_wts[...])

    spans = leads + leads % 2
    both = 2 * per

    def made_of(at):
        high, weight = hi_at[at, :], weight_at[at, :]
        low = jnp.sum(lo_at[at, :], 0, keepdims=True)
        left = jnp.concatenate(
            [jnp.where(high == float(i), weight, 0.0) for i in range(spans)], 0
        ).astype(jnp.bfloat16)
        digits = lax.broadcasted_iota(jnp.int32, (radix, radix), 0).astype(jnp.float32)
        right = jnp.where(digits == low, 1.0, 0.0).astype(jnp.bfloat16)
        return lax.dot_general(
            left, right, (((1,), (1,)), ((), ())), preferred_element_type=jnp.float32
        )

    def build(g):
        pair = [
            made_of(pl.ds(pl.multiple_of(g * both + i * per, per), per)) for i in range(2)
        ]
        at = pl.ds(pl.multiple_of(g * both, both), both)
        for i in range(leads):
            whole = jnp.concatenate([made[i * per:(i + 1) * per] for made in pair], 0)
            top = whole.astype(jnp.bfloat16)
            big[at, i * radix:(i + 1) * radix] = top
            small[at, i * radix:(i + 1) * radix] = (
                whole - top.astype(jnp.float32)
            ).astype(jnp.bfloat16)

    def share_copy(j, step, start, cut, passed=False):
        target, source = links[j]
        if passed:
            target, source = mate(0, beside), links[j - direct - 1][1]
        mine = slots.at[source if passed else doc, :, pl.ds(start, cut)]
        return pltpu.make_async_remote_copy(
            src_ref=mine, dst_ref=mine, send_sem=doc_send.at[j, step],
            recv_sem=doc_recv.at[j, step], device_id=(grp, target, voc),
            device_id_type=mesh_ids
        )

    def hand_on(step, start, cut):
        for j in range(direct + 1, len(links)):
            share_copy(j - direct - 1, step, start, cut).wait_recv()
            share_copy(j, step, start, cut, True).start()

    def decode(t, start, begin, cut, step, whole=False):
        tops = []
        for p in range(count):
            logits = jnp.dot(
                kept[p * length:(p + 1) * length, :], decoder[t, :, begin:begin + cut],
                preferred_element_type=jnp.float32
            )
            tops.append(jnp.max(logits, 0, keepdims=True))
        tops.append(jnp.zeros((pad - count, cut), jnp.float32))
        best = jnp.concatenate(tops, 0) + floor[pl.ds(start, cut)][None]
        slots[doc, :, pl.ds(start, cut)] = jnp.log1p(jnp.maximum(best, 0.0))
        for j in range(len(links) if whole else min(direct + 1, len(links))):
            share_copy(j, step, start, cut).start()

    rounds = queries // both
    steady = tiles - 1
    inner = rounds // max(steady, 1)

    def decode_tile(t, _):
        decoder_load(t).wait()
        for i in range(inner):
            build(t * inner + i)

        @pl.when(t == 0)
        def _():
            pl.semaphore_wait(barrier, len(links) + len(along))

        start = pl.multiple_of(t * tile, tile)
        decode(t, start, 0, tile, t)

        @pl.when(t > 0)
        def _():
            hand_on(t - 1, pl.multiple_of(start - tile, tile), tile)

        return 0

    lax.fori_loop(0, steady, decode_tile, 0)
    for g in range(inner * steady, rounds):
        build(g)
    decoder_load(steady).wait()
    cuts, begin = [], 0
    for i, cut in enumerate(pieces_of(tile)):
        start = steady * tile + begin
        whole = i > 0
        decode(steady, start, begin, cut, steady + i, whole)
        if i == 0:
            hand_on(steady - 1, start - tile, tile)
        cuts.append((steady + i, start, cut, not whole))
        begin += cut

    def contract(total, step, start, cut, passed):
        for j in range(len(links)):
            relay = passed and j > direct
            copy = share_copy(j, step, start, cut, relay)
            copy.wait_send()
            if not (passed and j < direct):
                copy.wait_recv()
        value = slots[:, :, pl.ds(start, cut)].reshape(docs * pad, cut)
        top = value.astype(jnp.bfloat16)
        rest = (value - top.astype(jnp.float32)).astype(jnp.bfloat16)
        pair = jnp.concatenate([top, rest], 0)
        for table in (big, small):
            total = total + lax.dot_general(
                pair, table[:, pl.ds(start, cut)], (((1,), (1,)), ((), ())),
                preferred_element_type=jnp.float32
            )
        return total

    total = jnp.zeros((2 * docs * pad, queries), jnp.float32)
    for t in range(steady):
        total = contract(total, t, t * tile, tile, True)
        if t == 0:
            hand_on(*cuts[0][:3])
    for cut in cuts:
        total = contract(total, *cut)
    total = (total[:docs * pad] + total[docs * pad:]) * score_scale
    part[...] = total.reshape(docs, pad, queries)

    share = docs // vocs
    copies = []
    for j, peer in enumerate(along):
        copy = pltpu.make_async_remote_copy(
            src_ref=part.at[pl.ds(peer[2] * share, share)], dst_ref=parts.at[j],
            send_sem=voc_send.at[j], recv_sem=voc_recv.at[j], device_id=peer,
            device_id_type=mesh_ids
        )
        copy.start()
        copies.append(copy)
    result = part[pl.ds(voc * share, share)]
    for j, copy in enumerate(copies):
        copy.wait()
        result = result + parts[j]
    for i in range(share):
        out[i * count:(i + 1) * count, :] = result[i, :count]


def shards(
    hidden, lengths, w_trans, b_trans, ln_gain, ln_bias, w_decode, b_decode, query_ids, query_wts
):
    docs, vocs = lax.axis_size("doc"), lax.axis_size("voc")
    count, length, features = hidden.shape
    width = w_decode.shape[1]
    tile = tile_of(width)
    tiles = width // tile
    steps = tiles - 1 + len(pieces_of(tile))
    terms = query_ids.shape[1]
    queries = query_ids.shape[0] // docs
    anywhere = pl.BlockSpec(memory_space=pl.ANY)
    inside = pl.BlockSpec(memory_space=pltpu.VMEM)
    lanes = pltpu.VMEM((queries, radix), jnp.float32)
    half = pltpu.VMEM((queries, width), jnp.bfloat16)
    row = pltpu.VMEM((features,), jnp.float32)
    queue = pltpu.SemaphoreType.DMA
    return pl.pallas_call(
        functools.partial(encode_kernel, (docs, vocs), count, tile),
        out_shape=jax.ShapeDtypeStruct((docs * count // vocs, queries), jnp.float32),
        in_specs=[anywhere] * 10,
        out_specs=inside,
        scratch_shapes=[
            pltpu.VMEM((count * length, features), jnp.bfloat16),
            pltpu.VMEM((features, features), jnp.bfloat16),
            pltpu.VMEM((tiles, features, tile), jnp.bfloat16),
            pltpu.VMEM((count * length, features), jnp.bfloat16),
            pltpu.VMEM((docs, pad, width), jnp.float32),
            pltpu.VMEM((terms, queries), jnp.int32),
            pltpu.VMEM((terms, queries), jnp.int32),
            lanes, lanes, lanes,
            half, half,
            pltpu.VMEM((docs, pad, queries), jnp.float32),
            pltpu.VMEM((vocs - 1, docs // vocs, pad, queries), jnp.float32),
            pltpu.SMEM((count,), jnp.int32),
            row, row, row,
            pltpu.VMEM((width,), jnp.float32),
            queue((8,)), queue((count,)), queue((tiles,)),
            queue((docs - 1, steps)), queue((docs - 1, steps)),
            queue((vocs - 1,)), queue((vocs - 1,)),
        ],
        compiler_params=pltpu.CompilerParams(
            collective_id=0, has_side_effects=True, vmem_limit_bytes=60 * 1024 * 1024
        ),
    )(
        lengths, b_trans, ln_gain, ln_bias, b_decode,
        hidden.reshape(count * length, features), w_trans, w_decode, query_ids.T, query_wts.T
    )


def solution(mesh):
    return jax.shard_map(
        shards,
        mesh=mesh,
        in_specs=(
            P(("grp", "doc"), None, None),
            P(("grp", "doc")),
            P(),
            P(),
            P(),
            P(),
            P(None, "voc"),
            P("voc"),
            P("grp", None),
            P("grp", None),
        ),
        out_specs=P(("grp", "voc"), "doc"),
        check_vma=False,
    )
```

```python
import functools

import jax
import jax.numpy as jnp
from jax import lax
from jax.experimental import pallas as pl
from jax.experimental.pallas import tpu as pltpu
from jax.sharding import PartitionSpec as P

eps = 1e-06
score_scale = 1.0 / 1024.0
radix = 256
pad = 8


def tile_of(width):
    best = 128
    for tile in range(128, 1537, 128):
        if width % tile == 0:
            best = tile
    return best


def pieces_of(tile):
    if tile < 768 or tile % 256:
        return [tile]
    first = tile // 512 * 256
    return [cut for cut in (first, tile - first - 256, 256) if cut]


def encode_kernel(
    sizes, count, tile, lens, b_trans, gain, bias, b_decode, hidden, w_trans, w_decode, ids, wts,
    out, states, mix, decoder, kept, slots, own_ids, own_wts, hi_at, lo_at, weight_at, big, small,
    part, parts, live, shift, scale, offset, floor,
    load_sem, state_sem, decoder_sem, doc_send, doc_recv, voc_send, voc_recv
):
    docs, vocs = sizes
    length, features = hidden.shape[0] // count, hidden.shape[1]
    width = w_decode.shape[1]
    tiles = width // tile
    slots_per, queries = own_ids.shape
    per = radix // slots_per
    leads = width // radix
    grp, doc, voc = (lax.axis_index(name) for name in ("grp", "doc", "voc"))
    mesh_ids = pl.DeviceIdType.MESH

    def state_load(p):
        rows = pl.ds(p * length, length)
        return pltpu.make_async_copy(hidden.at[rows], states.at[rows], state_sem.at[p])

    def decoder_load(t):
        cut = pl.ds(pl.multiple_of(t * tile, tile), tile)
        return pltpu.make_async_copy(w_decode.at[:, cut], decoder.at[t], decoder_sem.at[t])

    rows = pl.ds(pl.multiple_of(doc * queries, queries), queries)
    loads = [
        pltpu.make_async_copy(source, target, load_sem.at[i])
        for i, (source, target) in enumerate([
            (ids.at[:, rows], own_ids), (wts.at[:, rows], own_wts), (w_trans, mix),
            (lens, live), (b_trans, shift), (gain, scale), (bias, offset), (b_decode, floor),
        ])
    ]
    for load in loads[:3]:
        load.start()
    state_load(0).start()
    for load in loads[3:]:
        load.start()
    for p in range(1, count):
        state_load(p).start()

    cores = 2 - docs % 2
    chips = docs // cores
    chip, core = doc // cores, lax.rem(doc, cores)

    def mate(shift, side):
        return cores * lax.rem(chip + shift, chips) + side

    links = [
        [
            (mate(h, side), mate(chips - h, side))
            for side in ([core, cores - 1 - core] if cores == 2 else [core])
            if h or side is not core
        ]
        for h in range(chips)
    ]
    first_link = [sum(len(links[k]) for k in range(h)) for h in range(chips)]
    barrier = pltpu.get_barrier_semaphore()
    peers = [(grp, target, voc) for group in links for target, _ in group]
    along = [(grp, doc, lax.rem(voc + j, vocs)) for j in range(1, vocs)]
    for peer in peers + along:
        pl.semaphore_signal(barrier, inc=1, device_id=peer, device_id_type=mesh_ids)

    for load in loads[:2]:
        load.wait()
    local = own_ids[...] - voc * width
    lead = jnp.clip(local >> 8, -1, leads)
    spread_to = (
        lax.broadcasted_iota(jnp.int32, (slots_per, radix), 1) % slots_per
        == lax.broadcasted_iota(jnp.int32, (slots_per, radix), 0)
    ).astype(jnp.float32).astype(jnp.bfloat16)

    def widen(value):
        value = value.astype(jnp.float32).astype(jnp.bfloat16)
        return lax.dot_general(
            value, spread_to, (((0,), (0,)), ((), ())), preferred_element_type=jnp.float32
        )

    own = (
        lax.broadcasted_iota(jnp.int32, (queries, radix), 0) % per
        == lax.broadcasted_iota(jnp.int32, (queries, radix), 1) // slots_per
    )
    hi_at[...] = jnp.where(own, widen(lead), -1.0)
    lo_at[...] = jnp.where(own, widen(local & (radix - 1)), 0.0)
    weight_at[...] = widen(own_wts[...])
    for load in loads[2:]:
        load.wait()

    for p in range(count):
        state_load(p).wait()
        for t in range(p * tiles // count, (p + 1) * tiles // count):
            decoder_load(t).start()
        rows = pl.ds(p * length, length)
        pre = jnp.dot(states[rows, :], mix[...], preferred_element_type=jnp.float32)
        pre = pre + shift[...][None]
        twice = pre * (1.0 + lax.erf(pre * (0.5 ** 0.5)))
        centre = twice - jnp.mean(twice, -1, keepdims=True)
        spread = jnp.mean(centre * centre, -1, keepdims=True)
        normed = centre * lax.rsqrt(spread + 4.0 * eps) * scale[...][None] + offset[...][None]
        inside = lax.broadcasted_iota(jnp.int32, (length, features), 0) < live[p]
        kept[rows, :] = jnp.where(inside, normed, normed[0:1]).astype(jnp.bfloat16)

    spans = leads + leads % 2
    both = 2 * per

    def made_of(first):
        at = pl.ds(first, per)
        high, weight = hi_at[at, :], weight_at[at, :]
        low = jnp.sum(lo_at[at, :], 0, keepdims=True)
        left = jnp.concatenate(
            [jnp.where(high == float(i), weight, 0.0) for i in range(spans)], 0
        ).astype(jnp.bfloat16)
        digits = lax.broadcasted_iota(jnp.int32, (radix, radix), 0).astype(jnp.float32)
        right = jnp.where(digits == low, 1.0, 0.0).astype(jnp.bfloat16)
        return lax.dot_general(
            left, right, (((1,), (1,)), ((), ())), preferred_element_type=jnp.float32
        )

    def build(g):
        pair = [made_of(g * both + i * per) for i in range(2)]
        at = pl.ds(g * both, both)
        for i in range(leads):
            whole = jnp.concatenate([made[i * per:(i + 1) * per] for made in pair], 0)
            top = whole.astype(jnp.bfloat16)
            big[at, i * radix:(i + 1) * radix] = top
            small[at, i * radix:(i + 1) * radix] = (
                whole - top.astype(jnp.float32)
            ).astype(jnp.bfloat16)

    def share_copy(j, target, cut):
        step, start, size = cut
        mine = slots.at[doc, :, pl.ds(start, size)]
        return pltpu.make_async_remote_copy(
            src_ref=mine, dst_ref=mine, send_sem=doc_send.at[j, step],
            recv_sem=doc_recv.at[j, step], device_id=(grp, target, voc),
            device_id_type=mesh_ids
        )

    def arrive(h, cut):
        for j, (target, _) in enumerate(links[h]):
            share_copy(first_link[h] + j, target, cut).wait()

    def decode(t, begin, cut, between):
        step, start, size = cut
        tops = []
        for p in range(count):
            logits = jnp.dot(
                kept[p * length:(p + 1) * length, :], decoder[t, :, begin:begin + size],
                preferred_element_type=jnp.float32
            )
            tops.append(jnp.max(logits, 0, keepdims=True))
            if p == count // 2 and between is not None:
                between()
        tops.append(jnp.zeros((pad - count, size), jnp.float32))
        best = jnp.concatenate(tops, 0) + floor[pl.ds(start, size)][None]
        slots[doc, :, pl.ds(start, size)] = jnp.log1p(jnp.maximum(best, 0.0))
        for h in reversed(range(chips)):
            for j, (target, _) in enumerate(links[h]):
                share_copy(first_link[h] + j, target, cut).start()

    def contract(docs_at, many, cuts):
        total = jnp.zeros((2 * many * pad, queries), jnp.float32)
        for _, start, size in cuts:
            value = slots[docs_at, :, pl.ds(start, size)].reshape(many * pad, size)
            top = value.astype(jnp.bfloat16)
            rest = (value - top.astype(jnp.float32)).astype(jnp.bfloat16)
            pair = jnp.concatenate([top, rest], 0)
            for table in (big, small):
                total = total + lax.dot_general(
                    pair, table[:, pl.ds(start, size)], (((1,), (1,)), ((), ())),
                    preferred_element_type=jnp.float32
                )
        total = (total[:many * pad] + total[many * pad:]) * score_scale
        return total.reshape(many, pad, queries)

    rounds = queries // both
    early = max(1, min(2, tiles - 1))
    whole_tiles = [(t, t * tile, tile) for t in range(tiles - 1)]
    pieces, begin = [], (tiles - 1) * tile
    for size in pieces_of(tile):
        pieces.append((len(whole_tiles) + len(pieces), begin, size))
        begin += size
    part[...] = jnp.zeros_like(part)

    def add_all(cut):
        for h in range(chips):
            arrive(h, cut)
        part[...] += contract(pl.ds(0, docs), docs, [cut])

    ready = 0
    for t in range(tiles):
        decoder_load(t).wait()
        for g in range(rounds * t // early, rounds * (t + 1) // early):
            if t < early:
                build(g)
        if t == 0:
            pl.semaphore_wait(barrier, len(peers) + len(along))
        for i, cut in enumerate(whole_tiles[t:t + 1] or pieces):
            between = None
            if t >= 2 and t >= early and i == 0:
                between = functools.partial(add_all, whole_tiles[ready])
                ready += 1
            decode(t, cut[1] - t * tile, cut, between)

    share = docs // vocs
    for h in range(chips):
        for cut in whole_tiles[ready:] + pieces:
            arrive(h, cut)
        at = cores * lax.rem(chip + chips - h, chips)
        part[pl.ds(at, cores)] += contract(
            pl.ds(at, cores), cores, whole_tiles[ready:] + pieces
        )
        for i in range(cores):
            item = at + i
            goal = item // share
            hop = lax.rem(goal + vocs - voc, vocs)

            @pl.when(hop != 0)
            def _():
                pltpu.make_async_remote_copy(
                    src_ref=part.at[item], dst_ref=parts.at[hop - 1, lax.rem(item, share)],
                    send_sem=voc_send.at[hop - 1, lax.rem(item, share)],
                    recv_sem=voc_recv.at[hop - 1, lax.rem(item, share)],
                    device_id=(grp, doc, goal), device_id_type=mesh_ids
                ).start()

    result = part[pl.ds(voc * share, share)]
    for j, peer in enumerate(along):
        for i in range(share):
            pltpu.make_async_remote_copy(
                src_ref=part.at[peer[2] * share + i], dst_ref=parts.at[j, i],
                send_sem=voc_send.at[j, i], recv_sem=voc_recv.at[j, i], device_id=peer,
                device_id_type=mesh_ids
            ).wait()
        result = result + parts[j]
    for i in range(share):
        out[i * count:(i + 1) * count, :] = result[i, :count]


def shards(
    hidden, lengths, w_trans, b_trans, ln_gain, ln_bias, w_decode, b_decode, query_ids, query_wts
):
    docs, vocs = lax.axis_size("doc"), lax.axis_size("voc")
    count, length, features = hidden.shape
    width = w_decode.shape[1]
    tile = tile_of(width)
    tiles = width // tile
    steps = tiles - 1 + len(pieces_of(tile))
    terms = query_ids.shape[1]
    queries = query_ids.shape[0] // docs
    anywhere = pl.BlockSpec(memory_space=pl.ANY)
    inside = pl.BlockSpec(memory_space=pltpu.VMEM)
    lanes = pltpu.VMEM((queries, radix), jnp.float32)
    half = pltpu.VMEM((queries, width), jnp.bfloat16)
    row = pltpu.VMEM((features,), jnp.float32)
    queue = pltpu.SemaphoreType.DMA
    return pl.pallas_call(
        functools.partial(encode_kernel, (docs, vocs), count, tile),
        out_shape=jax.ShapeDtypeStruct((docs * count // vocs, queries), jnp.float32),
        in_specs=[anywhere] * 10,
        out_specs=inside,
        scratch_shapes=[
            pltpu.VMEM((count * length, features), jnp.bfloat16),
            pltpu.VMEM((features, features), jnp.bfloat16),
            pltpu.VMEM((tiles, features, tile), jnp.bfloat16),
            pltpu.VMEM((count * length, features), jnp.bfloat16),
            pltpu.VMEM((docs, pad, width), jnp.float32),
            pltpu.VMEM((terms, queries), jnp.int32),
            pltpu.VMEM((terms, queries), jnp.int32),
            lanes, lanes, lanes,
            half, half,
            pltpu.VMEM((docs, pad, queries), jnp.float32),
            pltpu.VMEM((vocs - 1, docs // vocs, pad, queries), jnp.float32),
            pltpu.SMEM((count,), jnp.int32),
            row, row, row,
            pltpu.VMEM((width,), jnp.float32),
            queue((8,)), queue((count,)), queue((tiles,)),
            queue((docs - 1, steps)), queue((docs - 1, steps)),
            queue((vocs - 1, docs // vocs)), queue((vocs - 1, docs // vocs)),
        ],
        compiler_params=pltpu.CompilerParams(
            collective_id=0, has_side_effects=True, vmem_limit_bytes=60 * 1024 * 1024
        ),
    )(
        lengths, b_trans, ln_gain, ln_bias, b_decode,
        hidden.reshape(count * length, features), w_trans, w_decode, query_ids.T, query_wts.T
    )


def solution(mesh):
    return jax.shard_map(
        shards,
        mesh=mesh,
        in_specs=(
            P(("grp", "doc"), None, None),
            P(("grp", "doc")),
            P(),
            P(),
            P(),
            P(),
            P(None, "voc"),
            P("voc"),
            P("grp", None),
            P("grp", None),
        ),
        out_specs=P(("grp", "voc"), "doc"),
        check_vma=False,
    )
```

```python
import functools

import jax
import jax.numpy as jnp
from jax import lax
from jax.experimental import pallas as pl
from jax.experimental.pallas import tpu as pltpu
from jax.sharding import PartitionSpec as P

eps = 1e-06
score_scale = 1.0 / 1024.0
radix = 256
pad = 8


def tile_of(width):
    best = 128
    for tile in range(128, 1537, 128):
        if width % tile == 0:
            best = tile
    return best


def pieces_of(tile):
    if tile < 768 or tile % 256:
        return [tile]
    first = tile // 512 * 256
    return [cut for cut in (first, tile - first - 256, 256) if cut]


def encode_kernel(
    sizes, count, tile, lens, b_trans, gain, bias, b_decode, hidden, w_trans, w_decode, ids, wts,
    out, states, mix, decoder, kept, slots, own_ids, own_wts, hi_at, lo_at, weight_at, big, small,
    part, parts, live, shift, scale, offset, floor,
    load_sem, state_sem, decoder_sem, doc_send, doc_recv, voc_send, voc_recv
):
    docs, vocs = sizes
    length, features = hidden.shape[0] // count, hidden.shape[1]
    width = w_decode.shape[1]
    tiles = width // tile
    slots_per, queries = own_ids.shape
    per = radix // slots_per
    leads = width // radix
    grp, doc, voc = (lax.axis_index(name) for name in ("grp", "doc", "voc"))
    mesh_ids = pl.DeviceIdType.MESH

    def state_load(p):
        rows = pl.ds(p * length, length)
        return pltpu.make_async_copy(hidden.at[rows], states.at[rows], state_sem.at[p])

    def decoder_load(t):
        cut = pl.ds(pl.multiple_of(t * tile, tile), tile)
        return pltpu.make_async_copy(w_decode.at[:, cut], decoder.at[t], decoder_sem.at[t])

    rows = pl.ds(pl.multiple_of(doc * queries, queries), queries)
    loads = [
        pltpu.make_async_copy(source, target, load_sem.at[i])
        for i, (source, target) in enumerate([
            (ids.at[:, rows], own_ids), (wts.at[:, rows], own_wts), (w_trans, mix),
            (lens, live), (b_trans, shift), (gain, scale), (bias, offset), (b_decode, floor),
        ])
    ]
    for load in loads[:3]:
        load.start()
    state_load(0).start()
    for load in loads[3:]:
        load.start()
    for p in range(1, count):
        state_load(p).start()

    cores = 2 - docs % 2
    chips = docs // cores
    chip, core = doc // cores, lax.rem(doc, cores)

    def mate(shift, side):
        return cores * lax.rem(chip + shift, chips) + side

    links = [
        [
            (mate(h, side), mate(chips - h, side))
            for side in ([core, cores - 1 - core] if cores == 2 else [core])
            if h or side is not core
        ]
        for h in range(chips)
    ]
    first_link = [sum(len(links[k]) for k in range(h)) for h in range(chips)]
    barrier = pltpu.get_barrier_semaphore()
    peers = [(grp, target, voc) for group in links for target, _ in group]
    along = [(grp, doc, lax.rem(voc + j, vocs)) for j in range(1, vocs)]
    for peer in peers + along:
        pl.semaphore_signal(barrier, inc=1, device_id=peer, device_id_type=mesh_ids)

    for load in loads[:2]:
        load.wait()
    local = own_ids[...] - voc * width
    lead = jnp.clip(local >> 8, -1, leads)
    spread_to = (
        lax.broadcasted_iota(jnp.int32, (slots_per, radix), 1) % slots_per
        == lax.broadcasted_iota(jnp.int32, (slots_per, radix), 0)
    ).astype(jnp.float32).astype(jnp.bfloat16)

    def widen(value):
        value = value.astype(jnp.float32).astype(jnp.bfloat16)
        return lax.dot_general(
            value, spread_to, (((0,), (0,)), ((), ())), preferred_element_type=jnp.float32
        )

    own = (
        lax.broadcasted_iota(jnp.int32, (queries, radix), 0) % per
        == lax.broadcasted_iota(jnp.int32, (queries, radix), 1) // slots_per
    )
    hi_at[...] = jnp.where(own, widen(lead), -1.0)
    lo_at[...] = jnp.where(own, widen(local & (radix - 1)), 0.0)
    weight_at[...] = widen(own_wts[...])
    for load in loads[2:]:
        load.wait()

    for p in range(count):
        for later in {0: range(min(2, count)), 2: range(2, count)}.get(p, ()):
            state_load(later).wait()
        for t in {0: range(min(2, tiles)), 2: range(2, tiles)}.get(p, ()):
            decoder_load(t).start()
        rows = pl.ds(p * length, length)
        pre = jnp.dot(states[rows, :], mix[...], preferred_element_type=jnp.float32)
        pre = pre + shift[...][None]
        twice = pre * (1.0 + lax.erf(pre * (0.5 ** 0.5)))
        centre = twice - jnp.mean(twice, -1, keepdims=True)
        spread = jnp.mean(centre * centre, -1, keepdims=True)
        normed = centre * lax.rsqrt(spread + 4.0 * eps) * scale[...][None] + offset[...][None]
        inside = lax.broadcasted_iota(jnp.int32, (length, features), 0) < live[p]
        kept[rows, :] = jnp.where(inside, normed, normed[0:1]).astype(jnp.bfloat16)

    spans = leads + leads % 2
    both = 2 * per

    def made_of(first):
        at = pl.ds(first, per)
        high, weight = hi_at[at, :], weight_at[at, :]
        low = jnp.sum(lo_at[at, :], 0, keepdims=True)
        left = jnp.concatenate(
            [jnp.where(high == float(i), weight, 0.0) for i in range(spans)], 0
        ).astype(jnp.bfloat16)
        digits = lax.broadcasted_iota(jnp.int32, (radix, radix), 0).astype(jnp.float32)
        right = jnp.where(digits == low, 1.0, 0.0).astype(jnp.bfloat16)
        return lax.dot_general(
            left, right, (((1,), (1,)), ((), ())), preferred_element_type=jnp.float32
        )

    def build(g):
        pair = [made_of(g * both + i * per) for i in range(2)]
        at = pl.ds(g * both, both)
        for i in range(leads):
            whole = jnp.concatenate([made[i * per:(i + 1) * per] for made in pair], 0)
            top = whole.astype(jnp.bfloat16)
            big[at, i * radix:(i + 1) * radix] = top
            small[at, i * radix:(i + 1) * radix] = (
                whole - top.astype(jnp.float32)
            ).astype(jnp.bfloat16)

    def share_copy(j, target, cut):
        step, start, size = cut
        mine = slots.at[doc, :, pl.ds(start, size)]
        return pltpu.make_async_remote_copy(
            src_ref=mine, dst_ref=mine, send_sem=doc_send.at[j, step],
            recv_sem=doc_recv.at[j, step], device_id=(grp, target, voc),
            device_id_type=mesh_ids
        )

    def arrive(h, cut):
        for j, (target, _) in enumerate(links[h]):
            share_copy(first_link[h] + j, target, cut).wait()

    def decode(t, begin, cut, between):
        step, start, size = cut
        tops = []
        for p in range(count):
            logits = jnp.dot(
                kept[p * length:(p + 1) * length, :], decoder[t, :, begin:begin + size],
                preferred_element_type=jnp.float32
            )
            tops.append(jnp.max(logits, 0, keepdims=True))
            if p == count // 2 and between is not None:
                between()
        tops.append(jnp.zeros((pad - count, size), jnp.float32))
        best = jnp.concatenate(tops, 0) + floor[pl.ds(start, size)][None]
        slots[doc, :, pl.ds(start, size)] = jnp.log1p(jnp.maximum(best, 0.0))
        for h in reversed(range(chips)):
            for j, (target, _) in enumerate(links[h]):
                share_copy(first_link[h] + j, target, cut).start()

    def contract(docs_at, many, cuts):
        total = jnp.zeros((2 * many * pad, queries), jnp.float32)
        for _, start, size in cuts:
            value = slots[docs_at, :, pl.ds(start, size)].reshape(many * pad, size)
            top = value.astype(jnp.bfloat16)
            rest = (value - top.astype(jnp.float32)).astype(jnp.bfloat16)
            pair = jnp.concatenate([top, rest], 0)
            for table in (big, small):
                total = total + lax.dot_general(
                    pair, table[:, pl.ds(start, size)], (((1,), (1,)), ((), ())),
                    preferred_element_type=jnp.float32
                )
        total = (total[:many * pad] + total[many * pad:]) * score_scale
        return total.reshape(many, pad, queries)

    rounds = queries // both
    early = max(1, min(2, tiles - 1))
    whole_tiles = [(t, t * tile, tile) for t in range(tiles - 1)]
    pieces, begin = [], (tiles - 1) * tile
    for size in pieces_of(tile):
        pieces.append((len(whole_tiles) + len(pieces), begin, size))
        begin += size
    part[...] = jnp.zeros_like(part)

    def add_all(cut):
        for h in range(chips):
            arrive(h, cut)
        part[...] += contract(pl.ds(0, docs), docs, [cut])

    def first_doc(h):
        return cores * lax.rem(chip + chips - h, chips)

    def add(h, cuts):
        for cut in cuts:
            arrive(h, cut)
        at = pl.ds(first_doc(h), cores)
        part[at] += contract(at, cores, cuts)

    ready = max(0, tiles - max(2, early))
    remain = whole_tiles[ready:]
    for t in range(tiles):
        decoder_load(t).wait()
        for g in range(rounds * t // early, rounds * (t + 1) // early):
            if t < early:
                build(g)
        if t == 0:
            pl.semaphore_wait(barrier, len(peers) + len(along))
        for i, cut in enumerate(whole_tiles[t:t + 1] or pieces):
            between = None
            if t >= max(2, early) and i == 0:
                between = functools.partial(add_all, whole_tiles[t - max(2, early)])
            if t == tiles - 1 and i == 1:
                between = functools.partial(add, 0, remain)
            decode(t, cut[1] - t * tile, cut, between)

    share = docs // vocs

    def give_out(h):
        for i in range(cores):
            item = first_doc(h) + i
            goal = item // share
            hop = lax.rem(goal + vocs - voc, vocs)

            @pl.when(hop != 0)
            def _():
                pltpu.make_async_remote_copy(
                    src_ref=part.at[item], dst_ref=parts.at[hop - 1, lax.rem(item, share)],
                    send_sem=voc_send.at[hop - 1, lax.rem(item, share)],
                    recv_sem=voc_recv.at[hop - 1, lax.rem(item, share)],
                    device_id=(grp, doc, goal), device_id_type=mesh_ids
                ).start()

    if len(pieces) == 1:
        add(0, remain)
    if len(pieces) > 1:
        add(0, pieces[:-1])
    for h in range(1, chips):
        add(h, remain)
    add(0, pieces[-1:])
    give_out(0)
    for h in range(1, chips):
        if len(pieces) > 1:
            add(h, pieces[:-1])
        add(h, pieces[-1:])
        give_out(h)

    result = part[pl.ds(voc * share, share)]
    for j, peer in enumerate(along):
        for i in range(share):
            pltpu.make_async_remote_copy(
                src_ref=part.at[peer[2] * share + i], dst_ref=parts.at[j, i],
                send_sem=voc_send.at[j, i], recv_sem=voc_recv.at[j, i], device_id=peer,
                device_id_type=mesh_ids
            ).wait()
        result = result + parts[j]
    for i in range(share):
        out[i * count:(i + 1) * count, :] = result[i, :count]


def shards(
    hidden, lengths, w_trans, b_trans, ln_gain, ln_bias, w_decode, b_decode, query_ids, query_wts
):
    docs, vocs = lax.axis_size("doc"), lax.axis_size("voc")
    count, length, features = hidden.shape
    width = w_decode.shape[1]
    tile = tile_of(width)
    tiles = width // tile
    steps = tiles - 1 + len(pieces_of(tile))
    terms = query_ids.shape[1]
    queries = query_ids.shape[0] // docs
    anywhere = pl.BlockSpec(memory_space=pl.ANY)
    inside = pl.BlockSpec(memory_space=pltpu.VMEM)
    lanes = pltpu.VMEM((queries, radix), jnp.float32)
    half = pltpu.VMEM((queries, width), jnp.bfloat16)
    row = pltpu.VMEM((features,), jnp.float32)
    queue = pltpu.SemaphoreType.DMA
    return pl.pallas_call(
        functools.partial(encode_kernel, (docs, vocs), count, tile),
        out_shape=jax.ShapeDtypeStruct((docs * count // vocs, queries), jnp.float32),
        in_specs=[anywhere] * 10,
        out_specs=inside,
        scratch_shapes=[
            pltpu.VMEM((count * length, features), jnp.bfloat16),
            pltpu.VMEM((features, features), jnp.bfloat16),
            pltpu.VMEM((tiles, features, tile), jnp.bfloat16),
            pltpu.VMEM((count * length, features), jnp.bfloat16),
            pltpu.VMEM((docs, pad, width), jnp.float32),
            pltpu.VMEM((terms, queries), jnp.int32),
            pltpu.VMEM((terms, queries), jnp.int32),
            lanes, lanes, lanes,
            half, half,
            pltpu.VMEM((docs, pad, queries), jnp.float32),
            pltpu.VMEM((vocs - 1, docs // vocs, pad, queries), jnp.float32),
            pltpu.SMEM((count,), jnp.int32),
            row, row, row,
            pltpu.VMEM((width,), jnp.float32),
            queue((8,)), queue((count,)), queue((tiles,)),
            queue((docs - 1, steps)), queue((docs - 1, steps)),
            queue((vocs - 1, docs // vocs)), queue((vocs - 1, docs // vocs)),
        ],
        compiler_params=pltpu.CompilerParams(
            collective_id=0, has_side_effects=True, vmem_limit_bytes=60 * 1024 * 1024
        ),
    )(
        lengths, b_trans, ln_gain, ln_bias, b_decode,
        hidden.reshape(count * length, features), w_trans, w_decode, query_ids.T, query_wts.T
    )


def solution(mesh):
    return jax.shard_map(
        shards,
        mesh=mesh,
        in_specs=(
            P(("grp", "doc"), None, None),
            P(("grp", "doc")),
            P(),
            P(),
            P(),
            P(),
            P(None, "voc"),
            P("voc"),
            P("grp", None),
            P("grp", None),
        ),
        out_specs=P(("grp", "voc"), "doc"),
        check_vma=False,
    )
```

```python
import functools

import jax
import jax.numpy as jnp
from jax import lax
from jax.experimental import pallas as pl
from jax.experimental.pallas import tpu as pltpu
from jax.sharding import PartitionSpec as P

eps = 1e-06
score_scale = 1.0 / 1024.0
radix = 256
pad = 8


def tile_of(width):
    best = 128
    for tile in range(128, 1537, 128):
        if width % tile == 0:
            best = tile
    return best


def pieces_of(tile):
    if tile < 768 or tile % 256:
        return [tile]
    first = tile // 512 * 256
    return [cut for cut in (first, tile - first - 256, 256) if cut]


def encode_kernel(
    sizes, count, tile, lens, b_trans, gain, bias, b_decode, hidden, w_trans, w_decode, ids, wts,
    out, states, mix, decoder, kept, slots, own_ids, own_wts, hi_at, lo_at, weight_at, big, small,
    part, parts, live, shift, scale, offset, floor,
    load_sem, state_sem, decoder_sem, doc_send, doc_recv, voc_send, voc_recv
):
    docs, vocs = sizes
    length, features = hidden.shape[0] // count, hidden.shape[1]
    width = w_decode.shape[1]
    tiles = width // tile
    slots_per, queries = own_ids.shape
    per = radix // slots_per
    leads = width // radix
    grp, doc, voc = (lax.axis_index(name) for name in ("grp", "doc", "voc"))
    mesh_ids = pl.DeviceIdType.MESH

    def state_load(p):
        rows = pl.ds(p * length, length)
        return pltpu.make_async_copy(hidden.at[rows], states.at[rows], state_sem.at[p])

    def decoder_load(t):
        cut = pl.ds(pl.multiple_of(t * tile, tile), tile)
        return pltpu.make_async_copy(w_decode.at[:, cut], decoder.at[t], decoder_sem.at[t])

    rows = pl.ds(pl.multiple_of(doc * queries, queries), queries)
    loads = [
        pltpu.make_async_copy(source, target, load_sem.at[i])
        for i, (source, target) in enumerate([
            (ids.at[:, rows], own_ids), (wts.at[:, rows], own_wts), (w_trans, mix),
            (lens, live), (b_trans, shift), (gain, scale), (bias, offset), (b_decode, floor),
        ])
    ]
    for load in loads[:3]:
        load.start()
    state_load(0).start()
    for load in loads[3:]:
        load.start()
    for p in range(1, count):
        state_load(p).start()

    cores = 2 - docs % 2
    chips = docs // cores
    chip, core = doc // cores, lax.rem(doc, cores)

    def mate(shift, side):
        return cores * lax.rem(chip + shift, chips) + side

    links = [
        [
            (mate(h, side), mate(chips - h, side))
            for side in ([core, cores - 1 - core] if cores == 2 else [core])
            if h or side is not core
        ]
        for h in range(chips)
    ]
    first_link = [sum(len(links[k]) for k in range(h)) for h in range(chips)]
    barrier = pltpu.get_barrier_semaphore()
    peers = [(grp, target, voc) for group in links for target, _ in group]
    along = [(grp, doc, lax.rem(voc + j, vocs)) for j in range(1, vocs)]
    for peer in peers + along:
        pl.semaphore_signal(barrier, inc=1, device_id=peer, device_id_type=mesh_ids)

    for load in loads[:2]:
        load.wait()
    local = own_ids[...] - voc * width
    lead = jnp.clip(local >> 8, -1, leads)
    spread_to = (
        lax.broadcasted_iota(jnp.int32, (slots_per, radix), 1) % slots_per
        == lax.broadcasted_iota(jnp.int32, (slots_per, radix), 0)
    ).astype(jnp.float32).astype(jnp.bfloat16)

    def widen(value):
        value = value.astype(jnp.float32).astype(jnp.bfloat16)
        return lax.dot_general(
            value, spread_to, (((0,), (0,)), ((), ())), preferred_element_type=jnp.float32
        )

    own = (
        lax.broadcasted_iota(jnp.int32, (queries, radix), 0) % per
        == lax.broadcasted_iota(jnp.int32, (queries, radix), 1) // slots_per
    )
    hi_at[...] = jnp.where(own, widen(lead), -1.0)
    lo_at[...] = jnp.where(own, widen(local & (radix - 1)), 0.0)
    weight_at[...] = widen(own_wts[...])
    for load in loads[2:]:
        load.wait()

    for p in range(count):
        for later in {0: range(min(2, count)), 2: range(2, count)}.get(p, ()):
            state_load(later).wait()
        for t in {0: range(min(2, tiles)), 2: range(2, tiles)}.get(p, ()):
            decoder_load(t).start()
        rows = pl.ds(p * length, length)
        pre = jnp.dot(states[rows, :], mix[...], preferred_element_type=jnp.float32)
        pre = pre + shift[...][None]
        twice = pre * (1.0 + lax.erf(pre * (0.5 ** 0.5)))
        centre = twice - jnp.mean(twice, -1, keepdims=True)
        spread = jnp.mean(centre * centre, -1, keepdims=True)
        normed = centre * lax.rsqrt(spread + 4.0 * eps) * scale[...][None] + offset[...][None]
        inside = lax.broadcasted_iota(jnp.int32, (length, features), 0) < live[p]
        kept[rows, :] = jnp.where(inside, normed, normed[0:1]).astype(jnp.bfloat16)

    spans = leads + leads % 2
    both = 2 * per

    def made_of(first):
        at = pl.ds(first, per)
        high, weight = hi_at[at, :], weight_at[at, :]
        low = jnp.sum(lo_at[at, :], 0, keepdims=True)
        left = jnp.concatenate(
            [jnp.where(high == float(i), weight, 0.0) for i in range(spans)], 0
        ).astype(jnp.bfloat16)
        digits = lax.broadcasted_iota(jnp.int32, (radix, radix), 0).astype(jnp.float32)
        right = jnp.where(digits == low, 1.0, 0.0).astype(jnp.bfloat16)
        return lax.dot_general(
            left, right, (((1,), (1,)), ((), ())), preferred_element_type=jnp.float32
        )

    def build(g):
        pair = [made_of(g * both + i * per) for i in range(2)]
        at = pl.ds(g * both, both)
        for i in range(leads):
            whole = jnp.concatenate([made[i * per:(i + 1) * per] for made in pair], 0)
            top = whole.astype(jnp.bfloat16)
            big[at, i * radix:(i + 1) * radix] = top
            small[at, i * radix:(i + 1) * radix] = (
                whole - top.astype(jnp.float32)
            ).astype(jnp.bfloat16)

    def share_copy(j, target, cut):
        step, start, size = cut
        mine = slots.at[doc, :, pl.ds(start, size)]
        return pltpu.make_async_remote_copy(
            src_ref=mine, dst_ref=mine, send_sem=doc_send.at[j, step],
            recv_sem=doc_recv.at[j, step], device_id=(grp, target, voc),
            device_id_type=mesh_ids
        )

    def arrive(h, cut):
        for j, (target, _) in enumerate(links[h]):
            share_copy(first_link[h] + j, target, cut).wait()

    def decode(t, begin, cut, between):
        step, start, size = cut
        tops = []
        for p in range(count):
            logits = jnp.dot(
                kept[p * length:(p + 1) * length, :], decoder[t, :, begin:begin + size],
                preferred_element_type=jnp.float32
            )
            tops.append(jnp.max(logits, 0, keepdims=True))
            if p == count // 2 and between is not None:
                between()
        tops.append(jnp.zeros((pad - count, size), jnp.float32))
        best = jnp.concatenate(tops, 0) + floor[pl.ds(start, size)][None]
        slots[doc, :, pl.ds(start, size)] = jnp.log1p(jnp.maximum(best, 0.0))
        for h in reversed(range(chips)):
            for j, (target, _) in enumerate(links[h]):
                share_copy(first_link[h] + j, target, cut).start()

    def contract(docs_at, many, cuts):
        total = jnp.zeros((2 * many * pad, queries), jnp.float32)
        for _, start, size in cuts:
            value = slots[docs_at, :, pl.ds(start, size)].reshape(many * pad, size)
            top = value.astype(jnp.bfloat16)
            rest = (value - top.astype(jnp.float32)).astype(jnp.bfloat16)
            pair = jnp.concatenate([top, rest], 0)
            for table in (big, small):
                total = total + lax.dot_general(
                    pair, table[:, pl.ds(start, size)], (((1,), (1,)), ((), ())),
                    preferred_element_type=jnp.float32
                )
        total = (total[:many * pad] + total[many * pad:]) * score_scale
        return total.reshape(many, pad, queries)

    rounds = queries // both
    early = max(1, min(2, tiles - 1))
    whole_tiles = [(t, t * tile, tile) for t in range(tiles - 1)]
    pieces, begin = [], (tiles - 1) * tile
    for size in pieces_of(tile):
        pieces.append((len(whole_tiles) + len(pieces), begin, size))
        begin += size
    part[...] = jnp.zeros_like(part)

    def add_all(cut):
        for h in range(chips):
            arrive(h, cut)
        part[...] += contract(pl.ds(0, docs), docs, [cut])

    def first_doc(h):
        return cores * lax.rem(chip + chips - h, chips)

    def add(first, many, cuts, h=None):
        for cut in cuts:
            if h is not None:
                arrive(h, cut)
        at = pl.ds(first, many)
        part[at] += contract(at, many, cuts)

    ready = max(0, tiles - max(2, early))
    remain = whole_tiles[ready:]
    for t in range(tiles):
        decoder_load(t).wait()
        for g in range(rounds * t // early, rounds * (t + 1) // early):
            if t < early:
                build(g)
        if t == 0:
            pl.semaphore_wait(barrier, len(peers) + len(along))
        for i, cut in enumerate(whole_tiles[t:t + 1] or pieces):
            between = None
            if t >= max(2, early) and i == 0:
                between = functools.partial(add_all, whole_tiles[t - max(2, early)])
            if t == tiles - 1 and i == 1:
                between = functools.partial(add, first_doc(0), cores, remain, 0)
            if t == tiles - 1 and i == 2:
                between = functools.partial(add, doc, 1, pieces[:-1])
            decode(t, cut[1] - t * tile, cut, between)

    share = docs // vocs

    def give_out(item):
        goal = item // share
        hop = lax.rem(goal + vocs - voc, vocs)

        @pl.when(hop != 0)
        def _():
            pltpu.make_async_remote_copy(
                src_ref=part.at[item], dst_ref=parts.at[hop - 1, lax.rem(item, share)],
                send_sem=voc_send.at[hop - 1, lax.rem(item, share)],
                recv_sem=voc_recv.at[hop - 1, lax.rem(item, share)],
                device_id=(grp, doc, goal), device_id_type=mesh_ids
            ).start()

    if len(pieces) < 2:
        add(first_doc(0), cores, remain, 0)
    if len(pieces) == 2:
        add(doc, 1, pieces[:-1])
    add(doc, 1, pieces[-1:])
    give_out(doc)
    if cores == 2 and len(pieces) > 1:
        add(mate(0, 1 - core), 1, pieces[:-1], 0)
    for h in range(1, chips):
        add(first_doc(h), cores, remain, h)
    if cores == 2:
        add(mate(0, 1 - core), 1, pieces[-1:], 0)
        give_out(mate(0, 1 - core))
    for h in range(1, chips):
        if len(pieces) > 1:
            add(first_doc(h), cores, pieces[:-1], h)
        add(first_doc(h), cores, pieces[-1:], h)
        for i in range(cores):
            give_out(first_doc(h) + i)

    result = part[pl.ds(voc * share, share)]
    for j, peer in enumerate(along):
        for i in range(share):
            pltpu.make_async_remote_copy(
                src_ref=part.at[peer[2] * share + i], dst_ref=parts.at[j, i],
                send_sem=voc_send.at[j, i], recv_sem=voc_recv.at[j, i], device_id=peer,
                device_id_type=mesh_ids
            ).wait()
        result = result + parts[j]
    for i in range(share):
        out[i * count:(i + 1) * count, :] = result[i, :count]


def shards(
    hidden, lengths, w_trans, b_trans, ln_gain, ln_bias, w_decode, b_decode, query_ids, query_wts
):
    docs, vocs = lax.axis_size("doc"), lax.axis_size("voc")
    count, length, features = hidden.shape
    width = w_decode.shape[1]
    tile = tile_of(width)
    tiles = width // tile
    steps = tiles - 1 + len(pieces_of(tile))
    terms = query_ids.shape[1]
    queries = query_ids.shape[0] // docs
    anywhere = pl.BlockSpec(memory_space=pl.ANY)
    inside = pl.BlockSpec(memory_space=pltpu.VMEM)
    lanes = pltpu.VMEM((queries, radix), jnp.float32)
    half = pltpu.VMEM((queries, width), jnp.bfloat16)
    row = pltpu.VMEM((features,), jnp.float32)
    queue = pltpu.SemaphoreType.DMA
    return pl.pallas_call(
        functools.partial(encode_kernel, (docs, vocs), count, tile),
        out_shape=pltpu.VMEM((docs * count // vocs, queries), jnp.float32),
        in_specs=[anywhere] * 10,
        out_specs=inside,
        scratch_shapes=[
            pltpu.VMEM((count * length, features), jnp.bfloat16),
            pltpu.VMEM((features, features), jnp.bfloat16),
            pltpu.VMEM((tiles, features, tile), jnp.bfloat16),
            pltpu.VMEM((count * length, features), jnp.bfloat16),
            pltpu.VMEM((docs, pad, width), jnp.float32),
            pltpu.VMEM((terms, queries), jnp.int32),
            pltpu.VMEM((terms, queries), jnp.int32),
            lanes, lanes, lanes,
            half, half,
            pltpu.VMEM((docs, pad, queries), jnp.float32),
            pltpu.VMEM((vocs - 1, docs // vocs, pad, queries), jnp.float32),
            pltpu.SMEM((count,), jnp.int32),
            row, row, row,
            pltpu.VMEM((width,), jnp.float32),
            queue((8,)), queue((count,)), queue((tiles,)),
            queue((docs - 1, steps)), queue((docs - 1, steps)),
            queue((vocs - 1, docs // vocs)), queue((vocs - 1, docs // vocs)),
        ],
        compiler_params=pltpu.CompilerParams(
            collective_id=0, has_side_effects=True, vmem_limit_bytes=60 * 1024 * 1024
        ),
    )(
        lengths, b_trans, ln_gain, ln_bias, b_decode,
        hidden.reshape(count * length, features), w_trans, w_decode, query_ids.T, query_wts.T
    )


def solution(mesh):
    return jax.shard_map(
        shards,
        mesh=mesh,
        in_specs=(
            P(("grp", "doc"), None, None),
            P(("grp", "doc")),
            P(),
            P(),
            P(),
            P(),
            P(None, "voc"),
            P("voc"),
            P("grp", None),
            P("grp", None),
        ),
        out_specs=P(("grp", "voc"), "doc"),
        check_vma=False,
    )
```

```python
import functools

import jax
import jax.numpy as jnp
from jax import lax
from jax.experimental import pallas as pl
from jax.experimental.pallas import tpu as pltpu
from jax.sharding import PartitionSpec as P

eps = 1e-06
score_scale = 1.0 / 1024.0
radix = 256
pad = 8


def tile_of(width):
    best = 128
    for tile in range(128, 1537, 128):
        if width % tile == 0:
            best = tile
    return best


def pieces_of(tile):
    if tile < 768 or tile % 256:
        return [tile]
    first = tile // 512 * 256
    return [cut for cut in (first, tile - first - 256, 256) if cut]


def encode_kernel(
    sizes, count, tile, lens, b_trans, gain, bias, b_decode, hidden, w_trans, w_decode, ids, wts,
    out, states, mix, decoder, kept, slots, own_ids, own_wts, hi_at, lo_at, weight_at, big, small,
    part, parts, live, shift, scale, offset, floor,
    load_sem, state_sem, decoder_sem, doc_send, doc_recv, voc_send, voc_recv
):
    docs, vocs = sizes
    length, features = hidden.shape[0] // count, hidden.shape[1]
    width = w_decode.shape[1]
    tiles = width // tile
    slots_per, queries = own_ids.shape
    per = radix // slots_per
    leads = width // radix
    grp, doc, voc = (lax.axis_index(name) for name in ("grp", "doc", "voc"))
    mesh_ids = pl.DeviceIdType.MESH

    def state_load(p):
        rows = pl.ds(p * length, length)
        return pltpu.make_async_copy(hidden.at[rows], states.at[rows], state_sem.at[p])

    def decoder_load(t):
        cut = pl.ds(pl.multiple_of(t * tile, tile), tile)
        return pltpu.make_async_copy(w_decode.at[:, cut], decoder.at[t], decoder_sem.at[t])

    rows = pl.ds(pl.multiple_of(doc * queries, queries), queries)
    loads = [
        pltpu.make_async_copy(source, target, load_sem.at[i])
        for i, (source, target) in enumerate([
            (ids.at[:, rows], own_ids), (wts.at[:, rows], own_wts), (w_trans, mix),
            (lens, live), (b_trans, shift), (gain, scale), (bias, offset), (b_decode, floor),
        ])
    ]
    for load in loads[:3]:
        load.start()
    state_load(0).start()
    for load in loads[3:]:
        load.start()
    for p in range(1, count):
        state_load(p).start()

    cores = 2 - docs % 2
    chips = docs // cores
    chip, core = doc // cores, lax.rem(doc, cores)

    def mate(shift, side):
        return cores * lax.rem(chip + shift, chips) + side

    links = [
        [
            (mate(h, side), mate(chips - h, side))
            for side in ([core, cores - 1 - core] if cores == 2 else [core])
            if h or side is not core
        ]
        for h in range(chips)
    ]
    first_link = [sum(len(links[k]) for k in range(h)) for h in range(chips)]
    barrier = pltpu.get_barrier_semaphore()
    peers = [(grp, target, voc) for group in links for target, _ in group]
    along = [(grp, doc, lax.rem(voc + j, vocs)) for j in range(1, vocs)]
    for peer in peers + along:
        pl.semaphore_signal(barrier, inc=1, device_id=peer, device_id_type=mesh_ids)

    for load in loads[:2]:
        load.wait()
    local = own_ids[...] - voc * width
    lead = jnp.clip(local >> 8, -1, leads)
    spread_to = (
        lax.broadcasted_iota(jnp.int32, (slots_per, radix), 1) % slots_per
        == lax.broadcasted_iota(jnp.int32, (slots_per, radix), 0)
    ).astype(jnp.float32).astype(jnp.bfloat16)

    def widen(value):
        value = value.astype(jnp.float32).astype(jnp.bfloat16)
        return lax.dot_general(
            value, spread_to, (((0,), (0,)), ((), ())), preferred_element_type=jnp.float32
        )

    own = (
        lax.broadcasted_iota(jnp.int32, (queries, radix), 0) % per
        == lax.broadcasted_iota(jnp.int32, (queries, radix), 1) // slots_per
    )
    hi_at[...] = jnp.where(own, widen(lead), -1.0)
    lo_at[...] = jnp.where(own, widen(local & (radix - 1)), 0.0)
    weight_at[...] = widen(own_wts[...])
    spans = leads + leads % 2
    both = 2 * per
    rounds = queries // both
    ahead = rounds * 8 // 16

    def made_of(first):
        at = pl.ds(first, per)
        high, weight = hi_at[at, :], weight_at[at, :]
        low = jnp.sum(lo_at[at, :], 0, keepdims=True)
        left = jnp.concatenate(
            [jnp.where(high == float(i), weight, 0.0) for i in range(spans)], 0
        ).astype(jnp.bfloat16)
        digits = lax.broadcasted_iota(jnp.int32, (radix, radix), 0).astype(jnp.float32)
        right = jnp.where(digits == low, 1.0, 0.0).astype(jnp.bfloat16)
        return lax.dot_general(
            left, right, (((1,), (1,)), ((), ())), preferred_element_type=jnp.float32
        )

    def build(g):
        pair = [made_of(g * both + i * per) for i in range(2)]
        at = pl.ds(g * both, both)
        for i in range(leads):
            whole = jnp.concatenate([made[i * per:(i + 1) * per] for made in pair], 0)
            top = whole.astype(jnp.bfloat16)
            big[at, i * radix:(i + 1) * radix] = top
            small[at, i * radix:(i + 1) * radix] = (
                whole - top.astype(jnp.float32)
            ).astype(jnp.bfloat16)

    for g in range(ahead):
        build(g)
    for load in loads[2:]:
        load.wait()

    for p in range(count):
        for later in {0: range(min(2, count)), 2: range(2, count)}.get(p, ()):
            state_load(later).wait()
        for t in {0: range(min(2, tiles)), 2: range(2, tiles)}.get(p, ()):
            decoder_load(t).start()
        rows = pl.ds(p * length, length)
        pre = jnp.dot(states[rows, :], mix[...], preferred_element_type=jnp.float32)
        pre = pre + shift[...][None]
        twice = pre * (1.0 + lax.erf(pre * (0.5 ** 0.5)))
        centre = twice - jnp.mean(twice, -1, keepdims=True)
        spread = jnp.mean(centre * centre, -1, keepdims=True)
        normed = centre * lax.rsqrt(spread + 4.0 * eps) * scale[...][None] + offset[...][None]
        inside = lax.broadcasted_iota(jnp.int32, (length, features), 0) < live[p]
        kept[rows, :] = jnp.where(inside, normed, normed[0:1]).astype(jnp.bfloat16)

    def share_copy(j, target, cut):
        step, start, size = cut
        mine = slots.at[doc, :, pl.ds(start, size)]
        return pltpu.make_async_remote_copy(
            src_ref=mine, dst_ref=mine, send_sem=doc_send.at[j, step],
            recv_sem=doc_recv.at[j, step], device_id=(grp, target, voc),
            device_id_type=mesh_ids
        )

    def arrive(h, cut):
        for j, (target, _) in enumerate(links[h]):
            share_copy(first_link[h] + j, target, cut).wait()

    def decode(t, begin, cut, between):
        step, start, size = cut
        tops = []
        for p in range(count):
            logits = jnp.dot(
                kept[p * length:(p + 1) * length, :], decoder[t, :, begin:begin + size],
                preferred_element_type=jnp.float32
            )
            tops.append(jnp.max(logits, 0, keepdims=True))
            if p == count // 2 and between is not None:
                between()
        tops.append(jnp.zeros((pad - count, size), jnp.float32))
        best = jnp.concatenate(tops, 0) + floor[pl.ds(start, size)][None]
        slots[doc, :, pl.ds(start, size)] = jnp.log1p(jnp.maximum(best, 0.0))
        for h in reversed(range(chips)):
            for j, (target, _) in enumerate(links[h]):
                share_copy(first_link[h] + j, target, cut).start()

    def contract(docs_at, many, cuts):
        total = jnp.zeros((2 * many * pad, queries), jnp.float32)
        for _, start, size in cuts:
            value = slots[docs_at, :, pl.ds(start, size)].reshape(many * pad, size)
            top = value.astype(jnp.bfloat16)
            rest = (value - top.astype(jnp.float32)).astype(jnp.bfloat16)
            pair = jnp.concatenate([top, rest], 0)
            for table in (big, small):
                total = total + lax.dot_general(
                    pair, table[:, pl.ds(start, size)], (((1,), (1,)), ((), ())),
                    preferred_element_type=jnp.float32
                )
        total = (total[:many * pad] + total[many * pad:]) * score_scale
        return total.reshape(many, pad, queries)

    early = max(1, min(2, tiles - 1))
    whole_tiles = [(t, t * tile, tile) for t in range(tiles - 1)]
    pieces, begin = [], (tiles - 1) * tile
    for size in pieces_of(tile):
        pieces.append((len(whole_tiles) + len(pieces), begin, size))
        begin += size
    part[...] = jnp.zeros_like(part)

    def add_all(cut):
        for h in range(chips):
            arrive(h, cut)
        part[...] += contract(pl.ds(0, docs), docs, [cut])

    def first_doc(h):
        return cores * lax.rem(chip + chips - h, chips)

    def add(first, many, cuts, h=None):
        for cut in cuts:
            if h is not None:
                arrive(h, cut)
        at = pl.ds(first, many)
        part[at] += contract(at, many, cuts)

    def add_before_last():
        add(first_doc(0), cores, pieces[:1], 0)
        add(doc, 1, pieces[1:-1])

    ready = max(0, tiles - max(2, early))
    remain = whole_tiles[ready:]
    for t in range(tiles):
        decoder_load(t).wait()
        for g in range(
            ahead + (rounds - ahead) * t // early, ahead + (rounds - ahead) * (t + 1) // early
        ):
            if t < early:
                build(g)
        if t == 0:
            pl.semaphore_wait(barrier, len(peers) + len(along))
        for i, cut in enumerate(whole_tiles[t:t + 1] or pieces):
            between = None
            if t >= max(2, early) and i == 0:
                between = functools.partial(add_all, whole_tiles[t - max(2, early)])
            if t == tiles - 1 and i == 1:
                between = functools.partial(add, first_doc(0), cores, remain, 0)
            if t == tiles - 1 and i == 2:
                between = add_before_last
            decode(t, cut[1] - t * tile, cut, between)

    share = docs // vocs

    def give_out(item):
        goal = item // share
        hop = lax.rem(goal + vocs - voc, vocs)

        @pl.when(hop != 0)
        def _():
            pltpu.make_async_remote_copy(
                src_ref=part.at[item], dst_ref=parts.at[hop - 1, lax.rem(item, share)],
                send_sem=voc_send.at[hop - 1, lax.rem(item, share)],
                recv_sem=voc_recv.at[hop - 1, lax.rem(item, share)],
                device_id=(grp, doc, goal), device_id_type=mesh_ids
            ).start()

    if len(pieces) < 2:
        add(first_doc(0), cores, remain, 0)
    joint = len(pieces) > 2
    add(doc, 1, pieces[-1:] if joint else pieces)
    give_out(doc)
    for h in range(1, chips):
        add(first_doc(h), cores, remain, h)
    if cores == 2:
        add(mate(0, 1 - core), 1, pieces[1:] if joint else pieces, 0)
        give_out(mate(0, 1 - core))
    for h in range(1, chips):
        if joint:
            add(first_doc(h), cores, pieces[:1], h)
        add(first_doc(h), cores, pieces[1:] if joint else pieces, h)
        for i in range(cores):
            give_out(first_doc(h) + i)

    result = part[pl.ds(voc * share, share)]
    for j, peer in enumerate(along):
        for i in range(share):
            pltpu.make_async_remote_copy(
                src_ref=part.at[peer[2] * share + i], dst_ref=parts.at[j, i],
                send_sem=voc_send.at[j, i], recv_sem=voc_recv.at[j, i], device_id=peer,
                device_id_type=mesh_ids
            ).wait()
        result = result + parts[j]
    for i in range(share):
        out[i * count:(i + 1) * count, :] = result[i, :count]


def shards(
    hidden, lengths, w_trans, b_trans, ln_gain, ln_bias, w_decode, b_decode, query_ids, query_wts
):
    docs, vocs = lax.axis_size("doc"), lax.axis_size("voc")
    count, length, features = hidden.shape
    width = w_decode.shape[1]
    tile = tile_of(width)
    tiles = width // tile
    steps = tiles - 1 + len(pieces_of(tile))
    terms = query_ids.shape[1]
    queries = query_ids.shape[0] // docs
    anywhere = pl.BlockSpec(memory_space=pl.ANY)
    inside = pl.BlockSpec(memory_space=pltpu.VMEM)
    lanes = pltpu.VMEM((queries, radix), jnp.float32)
    half = pltpu.VMEM((queries, width), jnp.bfloat16)
    row = pltpu.VMEM((features,), jnp.float32)
    queue = pltpu.SemaphoreType.DMA
    return pl.pallas_call(
        functools.partial(encode_kernel, (docs, vocs), count, tile),
        out_shape=pltpu.VMEM((docs * count // vocs, queries), jnp.float32),
        in_specs=[anywhere] * 10,
        out_specs=inside,
        scratch_shapes=[
            pltpu.VMEM((count * length, features), jnp.bfloat16),
            pltpu.VMEM((features, features), jnp.bfloat16),
            pltpu.VMEM((tiles, features, tile), jnp.bfloat16),
            pltpu.VMEM((count * length, features), jnp.bfloat16),
            pltpu.VMEM((docs, pad, width), jnp.float32),
            pltpu.VMEM((terms, queries), jnp.int32),
            pltpu.VMEM((terms, queries), jnp.int32),
            lanes, lanes, lanes,
            half, half,
            pltpu.VMEM((docs, pad, queries), jnp.float32),
            pltpu.VMEM((vocs - 1, docs // vocs, pad, queries), jnp.float32),
            pltpu.SMEM((count,), jnp.int32),
            row, row, row,
            pltpu.VMEM((width,), jnp.float32),
            queue((8,)), queue((count,)), queue((tiles,)),
            queue((docs - 1, steps)), queue((docs - 1, steps)),
            queue((vocs - 1, docs // vocs)), queue((vocs - 1, docs // vocs)),
        ],
        compiler_params=pltpu.CompilerParams(
            collective_id=0, has_side_effects=True, vmem_limit_bytes=60 * 1024 * 1024
        ),
    )(
        lengths, b_trans, ln_gain, ln_bias, b_decode,
        hidden.reshape(count * length, features), w_trans, w_decode, query_ids.T, query_wts.T
    )


def solution(mesh):
    return jax.shard_map(
        shards,
        mesh=mesh,
        in_specs=(
            P(("grp", "doc"), None, None),
            P(("grp", "doc")),
            P(),
            P(),
            P(),
            P(),
            P(None, "voc"),
            P("voc"),
            P("grp", None),
            P("grp", None),
        ),
        out_specs=P(("grp", "voc"), "doc"),
        check_vma=False,
    )
```

```python
import functools

import jax
import jax.numpy as jnp
from jax import lax
from jax.experimental import pallas as pl
from jax.experimental.pallas import tpu as pltpu
from jax.sharding import PartitionSpec as P

eps = 1e-06
score_scale = 1.0 / 1024.0
radix = 256
pad = 8


def tile_of(width):
    best = 128
    for tile in range(128, 1537, 128):
        if width % tile == 0:
            best = tile
    return best


def pieces_of(tile):
    if tile < 768 or tile % 256:
        return [tile]
    first = tile // 512 * 256
    return [cut for cut in (first, tile - first - 256, 256) if cut]


def encode_kernel(
    sizes, count, tile, lens, b_trans, gain, bias, b_decode, hidden, w_trans, w_decode, ids, wts,
    out, states, mix, decoder, kept, slots, own_ids, own_wts, hi_at, lo_at, weight_at, big, small,
    part, parts, live, shift, scale, offset, floor,
    load_sem, state_sem, decoder_sem, doc_send, doc_recv, voc_send, voc_recv
):
    docs, vocs = sizes
    length, features = hidden.shape[0] // count, hidden.shape[1]
    width = w_decode.shape[1]
    tiles = width // tile
    slots_per, queries = own_ids.shape
    per = radix // slots_per
    leads = width // radix
    grp, doc, voc = (lax.axis_index(name) for name in ("grp", "doc", "voc"))
    mesh_ids = pl.DeviceIdType.MESH

    def state_load(p):
        rows = pl.ds(p * length, length)
        return pltpu.make_async_copy(hidden.at[rows], states.at[rows], state_sem.at[p])

    def decoder_load(t):
        cut = pl.ds(pl.multiple_of(t * tile, tile), tile)
        return pltpu.make_async_copy(w_decode.at[:, cut], decoder.at[t], decoder_sem.at[t])

    rows = pl.ds(pl.multiple_of(doc * queries, queries), queries)
    loads = [
        pltpu.make_async_copy(source, target, load_sem.at[i])
        for i, (source, target) in enumerate([
            (ids.at[:, rows], own_ids), (wts.at[:, rows], own_wts), (w_trans, mix),
            (lens, live), (b_trans, shift), (gain, scale), (bias, offset), (b_decode, floor),
        ])
    ]
    for load in loads[:3]:
        load.start()
    state_load(0).start()
    for load in loads[3:]:
        load.start()
    for p in range(1, count):
        state_load(p).start()

    cores = 2 - docs % 2
    chips = docs // cores
    chip, core = doc // cores, lax.rem(doc, cores)

    def mate(shift, side):
        return cores * lax.rem(chip + shift, chips) + side

    links = [
        [
            (mate(h, side), mate(chips - h, side))
            for side in ([core, cores - 1 - core] if cores == 2 else [core])
            if h or side is not core
        ]
        for h in range(chips)
    ]
    first_link = [sum(len(links[k]) for k in range(h)) for h in range(chips)]
    barrier = pltpu.get_barrier_semaphore()
    peers = [(grp, target, voc) for group in links for target, _ in group]
    along = [(grp, doc, lax.rem(voc + j, vocs)) for j in range(1, vocs)]
    for peer in peers + along:
        pl.semaphore_signal(barrier, inc=1, device_id=peer, device_id_type=mesh_ids)

    for load in loads[:2]:
        load.wait()
    local = own_ids[...] - voc * width
    lead = jnp.clip(local >> 8, -1, leads)
    spread_to = (
        lax.broadcasted_iota(jnp.int32, (slots_per, radix), 1) % slots_per
        == lax.broadcasted_iota(jnp.int32, (slots_per, radix), 0)
    ).astype(jnp.float32).astype(jnp.bfloat16)

    def widen(value):
        value = value.astype(jnp.float32).astype(jnp.bfloat16)
        return lax.dot_general(
            value, spread_to, (((0,), (0,)), ((), ())), preferred_element_type=jnp.float32
        )

    own = (
        lax.broadcasted_iota(jnp.int32, (queries, radix), 0) % per
        == lax.broadcasted_iota(jnp.int32, (queries, radix), 1) // slots_per
    )
    hi_at[...] = jnp.where(own, widen(lead), -1.0)
    lo_at[...] = jnp.where(own, widen(local & (radix - 1)), 0.0)
    weight_at[...] = widen(own_wts[...])
    spans = leads + leads % 2
    both = 2 * per
    rounds = queries // both
    ahead = rounds * 8 // 16

    def made_of(first):
        at = pl.ds(first, per)
        high, weight = hi_at[at, :], weight_at[at, :]
        low = jnp.sum(lo_at[at, :], 0, keepdims=True)
        left = jnp.concatenate(
            [jnp.where(high == float(i), weight, 0.0) for i in range(spans)], 0
        ).astype(jnp.bfloat16)
        digits = lax.broadcasted_iota(jnp.int32, (radix, radix), 0).astype(jnp.float32)
        right = jnp.where(digits == low, 1.0, 0.0).astype(jnp.bfloat16)
        return lax.dot_general(
            left, right, (((1,), (1,)), ((), ())), preferred_element_type=jnp.float32
        )

    def build(g):
        pair = [made_of(g * both + i * per) for i in range(2)]
        at = pl.ds(g * both, both)
        for i in range(leads):
            whole = jnp.concatenate([made[i * per:(i + 1) * per] for made in pair], 0)
            top = whole.astype(jnp.bfloat16)
            big[at, i * radix:(i + 1) * radix] = top
            small[at, i * radix:(i + 1) * radix] = (
                whole - top.astype(jnp.float32)
            ).astype(jnp.bfloat16)

    for g in range(ahead):
        build(g)
    for load in loads[2:]:
        load.wait()

    for p in range(count):
        for later in {0: range(min(2, count)), 2: range(2, count)}.get(p, ()):
            state_load(later).wait()
        for t in {0: range(min(2, tiles)), 2: range(2, tiles)}.get(p, ()):
            decoder_load(t).start()
        rows = pl.ds(p * length, length)
        pre = jnp.dot(states[rows, :], mix[...], preferred_element_type=jnp.float32)
        pre = pre + shift[...][None]
        twice = pre * (1.0 + lax.erf(pre * (0.5 ** 0.5)))
        centre = twice - jnp.mean(twice, -1, keepdims=True)
        spread = jnp.mean(centre * centre, -1, keepdims=True)
        normed = centre * lax.rsqrt(spread + 4.0 * eps) * scale[...][None] + offset[...][None]
        inside = lax.broadcasted_iota(jnp.int32, (length, features), 0) < live[p]
        kept[rows, :] = jnp.where(inside, normed, normed[0:1]).astype(jnp.bfloat16)

    def share_copy(j, target, cut):
        step, start, size = cut
        mine = slots.at[doc, :, pl.ds(start, size)]
        return pltpu.make_async_remote_copy(
            src_ref=mine, dst_ref=mine, send_sem=doc_send.at[j, step],
            recv_sem=doc_recv.at[j, step], device_id=(grp, target, voc),
            device_id_type=mesh_ids
        )

    def arrive(h, cut):
        for j, (target, _) in enumerate(links[h]):
            share_copy(first_link[h] + j, target, cut).wait()

    def decode(t, begin, cut, between):
        step, start, size = cut
        tops = []
        for p in range(count):
            logits = jnp.dot(
                kept[p * length:(p + 1) * length, :], decoder[t, :, begin:begin + size],
                preferred_element_type=jnp.float32
            )
            tops.append(jnp.max(logits, 0, keepdims=True))
            if p == count // 2 and between is not None:
                between()
        tops.append(jnp.zeros((pad - count, size), jnp.float32))
        best = jnp.concatenate(tops, 0) + floor[pl.ds(start, size)][None]
        slots[doc, :, pl.ds(start, size)] = jnp.log1p(jnp.maximum(best, 0.0))
        for h in reversed(range(chips)):
            for j, (target, _) in enumerate(links[h]):
                share_copy(first_link[h] + j, target, cut).start()

    def contract(docs_at, many, cuts):
        total = jnp.zeros((2 * many * pad, queries), jnp.float32)
        for _, start, size in cuts:
            value = slots[docs_at, :, pl.ds(start, size)].reshape(many * pad, size)
            top = value.astype(jnp.bfloat16)
            rest = (value - top.astype(jnp.float32)).astype(jnp.bfloat16)
            pair = jnp.concatenate([top, rest], 0)
            for table in (big, small):
                total = total + lax.dot_general(
                    pair, table[:, pl.ds(start, size)], (((1,), (1,)), ((), ())),
                    preferred_element_type=jnp.float32
                )
        total = (total[:many * pad] + total[many * pad:]) * score_scale
        return total.reshape(many, pad, queries)

    early = max(1, min(2, tiles - 1))
    whole_tiles = [(t, t * tile, tile) for t in range(tiles - 1)]
    pieces, begin = [], (tiles - 1) * tile
    for size in pieces_of(tile):
        pieces.append((len(whole_tiles) + len(pieces), begin, size))
        begin += size
    part[...] = jnp.zeros_like(part)

    def add_all(cuts):
        for cut in cuts:
            for h in range(chips):
                arrive(h, cut)
        part[...] += contract(pl.ds(0, docs), docs, cuts)

    def first_doc(h):
        return cores * lax.rem(chip + chips - h, chips)

    def add(first, many, cuts, h=None):
        for cut in cuts:
            if h is not None:
                arrive(h, cut)
        at = pl.ds(first, many)
        part[at] += contract(at, many, cuts)

    def add_before_last():
        add(first_doc(0), cores, pieces[:1], 0)
        add(doc, 1, pieces[1:-1])

    ready = max(0, tiles - max(2, early))
    remain = whole_tiles[ready:]
    for t in range(tiles):
        decoder_load(t).wait()
        for g in range(
            ahead + (rounds - ahead) * t // early, ahead + (rounds - ahead) * (t + 1) // early
        ):
            if t < early:
                build(g)
        if t == 0:
            pl.semaphore_wait(barrier, len(peers) + len(along))
        for i, cut in enumerate(whole_tiles[t:t + 1] or pieces):
            between = None
            late = t - max(2, early)
            if i == 0 and late >= 0 and (late % 2 or t == tiles - 1):
                between = functools.partial(
                    add_all, whole_tiles[late - late % 2 if late % 2 else late:late + 1]
                )
            if t == tiles - 1 and i == 1:
                between = functools.partial(add, first_doc(0), cores, remain, 0)
            if t == tiles - 1 and i == 2:
                between = add_before_last
            decode(t, cut[1] - t * tile, cut, between)

    share = docs // vocs

    def give_out(item):
        goal = item // share
        hop = lax.rem(goal + vocs - voc, vocs)

        @pl.when(hop != 0)
        def _():
            pltpu.make_async_remote_copy(
                src_ref=part.at[item], dst_ref=parts.at[hop - 1, lax.rem(item, share)],
                send_sem=voc_send.at[hop - 1, lax.rem(item, share)],
                recv_sem=voc_recv.at[hop - 1, lax.rem(item, share)],
                device_id=(grp, doc, goal), device_id_type=mesh_ids
            ).start()

    if len(pieces) < 2:
        add(first_doc(0), cores, remain, 0)
    joint = len(pieces) > 2
    add(doc, 1, pieces[-1:] if joint else pieces)
    give_out(doc)
    for h in range(1, chips):
        add(first_doc(h), cores, remain, h)
    if cores == 2:
        add(mate(0, 1 - core), 1, pieces[1:] if joint else pieces, 0)
        give_out(mate(0, 1 - core))
    for h in range(1, chips):
        if joint:
            add(first_doc(h), cores, pieces[:1], h)
        last = pieces[1:] if joint else pieces
        for j, (target, source) in enumerate(links[h]):
            for cut in last:
                share_copy(first_link[h] + j, target, cut).wait()
            add(source, 1, last)
            give_out(source)

    result = part[pl.ds(voc * share, share)]
    for j, peer in enumerate(along):
        for i in range(share):
            pltpu.make_async_remote_copy(
                src_ref=part.at[peer[2] * share + i], dst_ref=parts.at[j, i],
                send_sem=voc_send.at[j, i], recv_sem=voc_recv.at[j, i], device_id=peer,
                device_id_type=mesh_ids
            ).wait()
        result = result + parts[j]
    for i in range(share):
        out[i * count:(i + 1) * count, :] = result[i, :count]


def shards(
    hidden, lengths, w_trans, b_trans, ln_gain, ln_bias, w_decode, b_decode, query_ids, query_wts
):
    docs, vocs = lax.axis_size("doc"), lax.axis_size("voc")
    count, length, features = hidden.shape
    width = w_decode.shape[1]
    tile = tile_of(width)
    tiles = width // tile
    steps = tiles - 1 + len(pieces_of(tile))
    terms = query_ids.shape[1]
    queries = query_ids.shape[0] // docs
    anywhere = pl.BlockSpec(memory_space=pl.ANY)
    inside = pl.BlockSpec(memory_space=pltpu.VMEM)
    lanes = pltpu.VMEM((queries, radix), jnp.float32)
    half = pltpu.VMEM((queries, width), jnp.bfloat16)
    row = pltpu.VMEM((features,), jnp.float32)
    queue = pltpu.SemaphoreType.DMA
    return pl.pallas_call(
        functools.partial(encode_kernel, (docs, vocs), count, tile),
        out_shape=pltpu.VMEM((docs * count // vocs, queries), jnp.float32),
        in_specs=[anywhere] * 10,
        out_specs=inside,
        scratch_shapes=[
            pltpu.VMEM((count * length, features), jnp.bfloat16),
            pltpu.VMEM((features, features), jnp.bfloat16),
            pltpu.VMEM((tiles, features, tile), jnp.bfloat16),
            pltpu.VMEM((count * length, features), jnp.bfloat16),
            pltpu.VMEM((docs, pad, width), jnp.float32),
            pltpu.VMEM((terms, queries), jnp.int32),
            pltpu.VMEM((terms, queries), jnp.int32),
            lanes, lanes, lanes,
            half, half,
            pltpu.VMEM((docs, pad, queries), jnp.float32),
            pltpu.VMEM((vocs - 1, docs // vocs, pad, queries), jnp.float32),
            pltpu.SMEM((count,), jnp.int32),
            row, row, row,
            pltpu.VMEM((width,), jnp.float32),
            queue((8,)), queue((count,)), queue((tiles,)),
            queue((docs - 1, steps)), queue((docs - 1, steps)),
            queue((vocs - 1, docs // vocs)), queue((vocs - 1, docs // vocs)),
        ],
        compiler_params=pltpu.CompilerParams(
            collective_id=0, has_side_effects=True, vmem_limit_bytes=60 * 1024 * 1024
        ),
    )(
        lengths, b_trans, ln_gain, ln_bias, b_decode,
        hidden.reshape(count * length, features), w_trans, w_decode, query_ids.T, query_wts.T
    )


def solution(mesh):
    return jax.shard_map(
        shards,
        mesh=mesh,
        in_specs=(
            P(("grp", "doc"), None, None),
            P(("grp", "doc")),
            P(),
            P(),
            P(),
            P(),
            P(None, "voc"),
            P("voc"),
            P("grp", None),
            P("grp", None),
        ),
        out_specs=P(("grp", "voc"), "doc"),
        check_vma=False,
    )
```

```python
import functools

import jax
import jax.numpy as jnp
from jax import lax
from jax.experimental import pallas as pl
from jax.experimental.pallas import tpu as pltpu
from jax.sharding import PartitionSpec as P

eps = 1e-06
score_scale = 1.0 / 1024.0
radix = 256
pad = 8


def tile_of(width):
    best = 128
    for tile in range(128, 1537, 128):
        if width % tile == 0:
            best = tile
    return best


def pieces_of(tile):
    if tile < 768 or tile % 256:
        return [tile]
    first = tile // 512 * 256
    return [cut for cut in (first, tile - first - 256, 256) if cut]


def encode_kernel(
    sizes, count, tile, lens, b_trans, gain, bias, b_decode, hidden, w_trans, w_decode, ids, wts,
    out, states, mix, decoder, kept, slots, own_ids, own_wts, hi_at, lo_at, weight_at, big, small,
    part, parts, live, shift, scale, offset, floor,
    load_sem, state_sem, decoder_sem, doc_send, doc_recv, voc_send, voc_recv
):
    docs, vocs = sizes
    length, features = hidden.shape[0] // count, hidden.shape[1]
    width = w_decode.shape[1]
    tiles = width // tile
    slots_per, queries = own_ids.shape
    per = radix // slots_per
    leads = width // radix
    grp, doc, voc = (lax.axis_index(name) for name in ("grp", "doc", "voc"))
    mesh_ids = pl.DeviceIdType.MESH

    def state_load(p):
        rows = pl.ds(p * length, length)
        return pltpu.make_async_copy(hidden.at[rows], states.at[rows], state_sem.at[p])

    def decoder_load(t):
        cut = pl.ds(pl.multiple_of(t * tile, tile), tile)
        return pltpu.make_async_copy(w_decode.at[:, cut], decoder.at[t], decoder_sem.at[t])

    rows = pl.ds(pl.multiple_of(doc * queries, queries), queries)
    loads = [
        pltpu.make_async_copy(source, target, load_sem.at[i])
        for i, (source, target) in enumerate([
            (ids.at[:, rows], own_ids), (wts.at[:, rows], own_wts), (w_trans, mix),
            (lens, live), (b_trans, shift), (gain, scale), (bias, offset), (b_decode, floor),
        ])
    ]
    for load in loads[:3]:
        load.start()
    state_load(0).start()
    for load in loads[3:]:
        load.start()
    for p in range(1, count):
        state_load(p).start()

    cores = 2 - docs % 2
    chips = docs // cores
    chip, core = doc // cores, lax.rem(doc, cores)

    def mate(shift, side):
        return cores * lax.rem(chip + shift, chips) + side

    links = [
        [
            (mate(h, side), mate(chips - h, side))
            for side in ([core, cores - 1 - core] if cores == 2 else [core])
            if h or side is not core
        ]
        for h in range(chips)
    ]
    first_link = [sum(len(links[k]) for k in range(h)) for h in range(chips)]
    barrier = pltpu.get_barrier_semaphore()
    peers = [(grp, target, voc) for group in links for target, _ in group]
    along = [(grp, doc, lax.rem(voc + j, vocs)) for j in range(1, vocs)]
    for peer in peers + along:
        pl.semaphore_signal(barrier, inc=1, device_id=peer, device_id_type=mesh_ids)

    for load in loads[:2]:
        load.wait()
    local = own_ids[...] - voc * width
    lead = jnp.clip(local >> 8, -1, leads)
    spread_to = (
        lax.broadcasted_iota(jnp.int32, (slots_per, radix), 1) % slots_per
        == lax.broadcasted_iota(jnp.int32, (slots_per, radix), 0)
    ).astype(jnp.float32).astype(jnp.bfloat16)

    def widen(value):
        value = value.astype(jnp.float32).astype(jnp.bfloat16)
        return lax.dot_general(
            value, spread_to, (((0,), (0,)), ((), ())), preferred_element_type=jnp.float32
        )

    own = (
        lax.broadcasted_iota(jnp.int32, (queries, radix), 0) % per
        == lax.broadcasted_iota(jnp.int32, (queries, radix), 1) // slots_per
    )
    hi_at[...] = jnp.where(own, widen(lead), -1.0)
    lo_at[...] = jnp.where(own, widen(local & (radix - 1)), 0.0)
    weight_at[...] = widen(own_wts[...])
    spans = leads + leads % 2
    both = 2 * per
    rounds = queries // both
    ahead = rounds * 8 // 16

    def made_of(first):
        at = pl.ds(first, per)
        high, weight = hi_at[at, :], weight_at[at, :]
        low = jnp.sum(lo_at[at, :], 0, keepdims=True)
        left = jnp.concatenate(
            [jnp.where(high == float(i), weight, 0.0) for i in range(spans)], 0
        ).astype(jnp.bfloat16)
        digits = lax.broadcasted_iota(jnp.int32, (radix, radix), 0).astype(jnp.float32)
        right = jnp.where(digits == low, 1.0, 0.0).astype(jnp.bfloat16)
        return lax.dot_general(
            left, right, (((1,), (1,)), ((), ())), preferred_element_type=jnp.float32
        )

    def build(g):
        pair = [made_of(g * both + i * per) for i in range(2)]
        at = pl.ds(g * both, both)
        for i in range(leads):
            whole = jnp.concatenate([made[i * per:(i + 1) * per] for made in pair], 0)
            top = whole.astype(jnp.bfloat16)
            big[at, i * radix:(i + 1) * radix] = top
            small[at, i * radix:(i + 1) * radix] = (
                whole - top.astype(jnp.float32)
            ).astype(jnp.bfloat16)

    for g in range(ahead):
        build(g)
    for load in loads[2:]:
        load.wait()

    for p in range(count):
        for later in {0: range(min(2, count)), 2: range(2, count)}.get(p, ()):
            state_load(later).wait()
        for t in {0: range(min(2, tiles)), 2: range(2, tiles)}.get(p, ()):
            decoder_load(t).start()
        rows = pl.ds(p * length, length)
        pre = jnp.dot(states[rows, :], mix[...], preferred_element_type=jnp.float32)
        pre = pre + shift[...][None]
        twice = pre * (1.0 + lax.erf(pre * (0.5 ** 0.5)))
        centre = twice - jnp.mean(twice, -1, keepdims=True)
        spread = jnp.mean(centre * centre, -1, keepdims=True)
        normed = centre * lax.rsqrt(spread + 4.0 * eps) * scale[...][None] + offset[...][None]
        inside = lax.broadcasted_iota(jnp.int32, (length, features), 0) < live[p]
        kept[rows, :] = jnp.where(inside, normed, normed[0:1]).astype(jnp.bfloat16)

    def share_copy(j, target, cut):
        step, start, size = cut
        mine = slots.at[doc, :, pl.ds(start, size)]
        return pltpu.make_async_remote_copy(
            src_ref=mine, dst_ref=mine, send_sem=doc_send.at[j, step],
            recv_sem=doc_recv.at[j, step], device_id=(grp, target, voc),
            device_id_type=mesh_ids
        )

    def arrive(h, cut):
        for j, (target, _) in enumerate(links[h]):
            share_copy(first_link[h] + j, target, cut).wait()

    def decode(t, begin, cut, between):
        step, start, size = cut
        tops = []
        for p in range(count):
            logits = jnp.dot(
                kept[p * length:(p + 1) * length, :], decoder[t, :, begin:begin + size],
                preferred_element_type=jnp.float32
            )
            tops.append(jnp.max(logits, 0, keepdims=True))
            if p == count // 2 and between is not None:
                between()
        tops.append(jnp.zeros((pad - count, size), jnp.float32))
        best = jnp.concatenate(tops, 0) + floor[pl.ds(start, size)][None]
        slots[doc, :, pl.ds(start, size)] = jnp.log1p(jnp.maximum(best, 0.0))
        for h in reversed(range(chips)):
            for j, (target, _) in enumerate(links[h]):
                share_copy(first_link[h] + j, target, cut).start()

    def contract(docs_at, many, cuts):
        total = jnp.zeros((2 * many * pad, queries), jnp.float32)
        for _, start, size in cuts:
            value = slots[docs_at, :, pl.ds(start, size)].reshape(many * pad, size)
            top = value.astype(jnp.bfloat16)
            rest = (value - top.astype(jnp.float32)).astype(jnp.bfloat16)
            pair = jnp.concatenate([top, rest], 0)
            for table in (big, small):
                total = total + lax.dot_general(
                    pair, table[:, pl.ds(start, size)], (((1,), (1,)), ((), ())),
                    preferred_element_type=jnp.float32
                )
        total = (total[:many * pad] + total[many * pad:]) * score_scale
        return total.reshape(many, pad, queries)

    early = max(1, min(2, tiles - 1))
    whole_tiles = [(t, t * tile, tile) for t in range(tiles - 1)]
    pieces, begin = [], (tiles - 1) * tile
    for size in pieces_of(tile):
        pieces.append((len(whole_tiles) + len(pieces), begin, size))
        begin += size
    part[...] = jnp.zeros_like(part)

    def add_all(cuts):
        for cut in cuts:
            for h in range(chips):
                arrive(h, cut)
        part[...] += contract(pl.ds(0, docs), docs, cuts)

    def first_doc(h):
        return cores * lax.rem(chip + chips - h, chips)

    def add(first, many, cuts, h=None):
        for cut in cuts:
            if h is not None:
                arrive(h, cut)
        at = pl.ds(first, many)
        part[at] += contract(at, many, cuts)

    def add_before_last():
        add(first_doc(0), cores, pieces[:1], 0)
        add(doc, 1, pieces[1:-1])

    ready = max(0, tiles - max(2, early))
    remain = whole_tiles[ready:]
    for t in range(tiles):
        decoder_load(t).wait()
        for g in range(
            ahead + (rounds - ahead) * t // early, ahead + (rounds - ahead) * (t + 1) // early
        ):
            if t < early:
                build(g)
        if t == 0:
            pl.semaphore_wait(barrier, len(peers) + len(along))
        for i, cut in enumerate(whole_tiles[t:t + 1] or pieces):
            between = None
            late = t - max(2, early)
            if i == 0 and late >= 0 and (late % 2 or t == tiles - 1):
                between = functools.partial(
                    add_all, whole_tiles[late - late % 2 if late % 2 else late:late + 1]
                )
            if t == tiles - 1 and i == 1:
                between = functools.partial(add, first_doc(0), cores, remain, 0)
            if t == tiles - 1 and i == 2:
                between = add_before_last
            decode(t, cut[1] - t * tile, cut, between)

    share = docs // vocs

    def give_out(item):
        goal = item // share
        hop = lax.rem(goal + vocs - voc, vocs)

        @pl.when(hop != 0)
        def _():
            pltpu.make_async_remote_copy(
                src_ref=part.at[item], dst_ref=parts.at[hop - 1, lax.rem(item, share)],
                send_sem=voc_send.at[hop - 1, lax.rem(item, share)],
                recv_sem=voc_recv.at[hop - 1, lax.rem(item, share)],
                device_id=(grp, doc, goal), device_id_type=mesh_ids
            ).start()

    if len(pieces) < 2:
        add(first_doc(0), cores, remain, 0)
    joint = len(pieces) > 2
    add(doc, 1, pieces[-1:] if joint else pieces)
    give_out(doc)
    for h in range(1, chips):
        add(first_doc(h), cores, remain + pieces[:1] if joint else remain, h)
    if cores == 2:
        add(mate(0, 1 - core), 1, pieces[1:] if joint else pieces, 0)
        give_out(mate(0, 1 - core))
    for h in range(1, chips):
        last = pieces[1:] if joint else pieces
        for j, (target, source) in enumerate(links[h]):
            for cut in last:
                share_copy(first_link[h] + j, target, cut).wait()
            add(source, 1, last)
            give_out(source)

    result = part[pl.ds(voc * share, share)]
    for j, peer in enumerate(along):
        for i in range(share):
            pltpu.make_async_remote_copy(
                src_ref=part.at[peer[2] * share + i], dst_ref=parts.at[j, i],
                send_sem=voc_send.at[j, i], recv_sem=voc_recv.at[j, i], device_id=peer,
                device_id_type=mesh_ids
            ).wait()
        result = result + parts[j]
    for i in range(share):
        out[i * count:(i + 1) * count, :] = result[i, :count]


def shards(
    hidden, lengths, w_trans, b_trans, ln_gain, ln_bias, w_decode, b_decode, query_ids, query_wts
):
    docs, vocs = lax.axis_size("doc"), lax.axis_size("voc")
    count, length, features = hidden.shape
    width = w_decode.shape[1]
    tile = tile_of(width)
    tiles = width // tile
    steps = tiles - 1 + len(pieces_of(tile))
    terms = query_ids.shape[1]
    queries = query_ids.shape[0] // docs
    anywhere = pl.BlockSpec(memory_space=pl.ANY)
    inside = pl.BlockSpec(memory_space=pltpu.VMEM)
    lanes = pltpu.VMEM((queries, radix), jnp.float32)
    half = pltpu.VMEM((queries, width), jnp.bfloat16)
    row = pltpu.VMEM((features,), jnp.float32)
    queue = pltpu.SemaphoreType.DMA
    return pl.pallas_call(
        functools.partial(encode_kernel, (docs, vocs), count, tile),
        out_shape=pltpu.VMEM((docs * count // vocs, queries), jnp.float32),
        in_specs=[anywhere] * 10,
        out_specs=inside,
        scratch_shapes=[
            pltpu.VMEM((count * length, features), jnp.bfloat16),
            pltpu.VMEM((features, features), jnp.bfloat16),
            pltpu.VMEM((tiles, features, tile), jnp.bfloat16),
            pltpu.VMEM((count * length, features), jnp.bfloat16),
            pltpu.VMEM((docs, pad, width), jnp.float32),
            pltpu.VMEM((terms, queries), jnp.int32),
            pltpu.VMEM((terms, queries), jnp.int32),
            lanes, lanes, lanes,
            half, half,
            pltpu.VMEM((docs, pad, queries), jnp.float32),
            pltpu.VMEM((vocs - 1, docs // vocs, pad, queries), jnp.float32),
            pltpu.SMEM((count,), jnp.int32),
            row, row, row,
            pltpu.VMEM((width,), jnp.float32),
            queue((8,)), queue((count,)), queue((tiles,)),
            queue((docs - 1, steps)), queue((docs - 1, steps)),
            queue((vocs - 1, docs // vocs)), queue((vocs - 1, docs // vocs)),
        ],
        compiler_params=pltpu.CompilerParams(
            collective_id=0, has_side_effects=True, vmem_limit_bytes=60 * 1024 * 1024
        ),
    )(
        lengths, b_trans, ln_gain, ln_bias, b_decode,
        hidden.reshape(count * length, features), w_trans, w_decode, query_ids.T, query_wts.T
    )


def solution(mesh):
    return jax.shard_map(
        shards,
        mesh=mesh,
        in_specs=(
            P(("grp", "doc"), None, None),
            P(("grp", "doc")),
            P(),
            P(),
            P(),
            P(),
            P(None, "voc"),
            P("voc"),
            P("grp", None),
            P("grp", None),
        ),
        out_specs=P(("grp", "voc"), "doc"),
        check_vma=False,
    )
```
